512 devices in a mesh: row: 16 (over z_hi, x), col: 32 (over z_lo, y, core).
Axes of the slice: x: 4, y: 8, z: 8 (z_hi: 4, z_lo: 2; z = z_hi * 2 + z_lo), core: 2. Of those that a mesh axis runs over, the one named last changes fastest.
Arguments:
- query_sketches: bfloat16 [512, 16384], P('row', 'col'), may hold values from -200 to 200
- fisher_inverse: bfloat16 [16384, 16384], P('row', 'col'), may hold values from -1 to 3, as said below
- index_tiles: bfloat16 [32768, 16384], P('col', 'row'), may hold values from -6 to 6
Outputs:
- scores: float32 [512, 32768], P('row', 'col')
The draws below stay inside these ranges and needn't reach their ends.
Inputs may be any that keep to these rules, and one draw needn't show every extreme that they name: `fisher_inverse`: symmetric.
All inputs are finite; a program needn't handle non-finite values.
Results may differ from the reference program's by a relative error of at most 0.0029.
Values may be sent and summed in bfloat16 or wider, within the bound.
No kernel may reach another device: no remote copies, remote signals or barrier semaphores. Data moves between devices by JAX's collectives and lax.ppermute only.
A program may use at most 64 MiB of HBM per device.

```python
import math
import jax
import jax.numpy as jnp
from jax import lax

F = 16384
QB = 512
ROWS = 32768


def draw_query_sketches(key, part):
    keys = jax.random.split(jax.random.fold_in(key, 23), 3)
    base = jnp.clip(jax.random.normal(keys[0], (QB, F), jnp.float32), -6.0, 6.0)
    scales = jnp.exp(jax.random.uniform(keys[1], (QB, 1), jnp.float32, 0.0, math.log(10.0)))
    columns = jax.random.uniform(keys[2], (1, F), jnp.float32, 0.5, 1.5)
    return jnp.clip(base * scales * columns, -200.0, 200.0).astype(jnp.bfloat16)


def draw_fisher_inverse(key, part):
    keys = jax.random.split(jax.random.fold_in(key, 11), 2)
    noise = jnp.clip(jax.random.normal(keys[0], (F, F), jnp.float32), -6.0, 6.0)
    noise = noise * F ** (-0.5)
    ramp = jnp.arange(F).astype(jnp.float32) / F
    damping = (0.5 + 1.5 * ramp) * jax.random.uniform(keys[1], (F,), jnp.float32, 0.7, 1.4)
    matrix = 0.5 * (noise + noise.T)
    places = jnp.arange(F)
    return matrix.at[places, places].add(damping).astype(jnp.bfloat16)


def block_scale(stream_key, dims, cuts, low, top_value):
    level, own = 1.0, jax.random.fold_in(stream_key, 6)
    for dim, parts in cuts:
        steps = jnp.exp(jax.random.uniform(jax.random.fold_in(own, dim), (parts,), jnp.float32, low / len(cuts), top_value / len(cuts)))
        level = level * jnp.repeat(steps, dims[dim] // parts).reshape([-1 if axis == dim else 1 for axis in range(len(dims))])
    return level


def normal_values(rng, extent, scale, limit, shards=(), dtype=jnp.bfloat16):
    drawn = jax.random.normal(rng, extent, jnp.float32) * scale
    if len(shards) > 0:
        drawn = block_scale(rng, extent, shards, -0.22, 0.18) * drawn
    return jnp.clip(drawn, min=-limit, max=limit).astype(dtype)


def setup_inputs(seed: int = 0) -> dict:
    key_of = jax.random.split(jax.random.key(seed), 4)
    return {
        "query_sketches": draw_query_sketches(jax.random.fold_in(key_of[3], 71), 0),
        "fisher_inverse": draw_fisher_inverse(jax.random.fold_in(key_of[3], 71), 0),
        "index_tiles": normal_values(key_of[2], (ROWS, F), 1.0, 6.0, ((0, 32), (1, 16))),
    }


def reference(query_sketches, fisher_inverse, index_tiles):
    preconditioned = jnp.dot(query_sketches, fisher_inverse, preferred_element_type=jnp.float32)
    squares = lax.optimization_barrier(jnp.sum(preconditioned * preconditioned, axis=1, keepdims=True))
    unit_sketch = (preconditioned / jnp.sqrt(squares + 1e-06)).astype(jnp.bfloat16)
    return jnp.dot(unit_sketch, index_tiles.T, preferred_element_type=jnp.float32)
```

```python
import functools

import jax
import jax.numpy as jnp
from jax import lax
from jax.experimental import pallas as pl
from jax.experimental.pallas import tpu as pltpu
from jax.sharding import Mesh, PartitionSpec as P

F32, F16, BF16 = jnp.float32, jnp.float16, jnp.bfloat16
AXES = ("zh", "x", "zl", "y", "k")
ROW = ("zh", "x")
PAIR = ("zl", "y")
LANES = 128
VMEM, SMEM = pltpu.VMEM, pltpu.SMEM


def exponent(rows):
    top = jnp.max(jnp.abs(rows), axis=-1, keepdims=True)
    return jnp.clip(jnp.ceil(jnp.log2(jnp.maximum(top, 1e-30))), -100.0, 100.0)


def columns(height, *values):
    lane = lax.broadcasted_iota(jnp.int32, (height, LANES), 1)
    out = jnp.zeros((height, LANES), F32)
    for place, value in enumerate(values):
        out = jnp.where(lane == place, value, out)
    return out


def pieces(value):
    out = []
    for _ in range(3):
        out.append(value.astype(BF16).astype(F32))
        value = value - out[-1]
    return out


def dot_t(a, b):
    return lax.dot_general(a, b, (((1,), (1,)), ((), ())), preferred_element_type=F32)


def first_kernel(order, me, held, fisher, other, out):
    core = me[0]
    groups, _, height, width = held.shape
    mine = held[:, core].reshape(groups * height, width)
    theirs = held[:, 1 - core].reshape(groups * height, width)
    part = dot_t(mine, fisher[...]) + dot_t(theirs, other[...])
    features = part.shape[1]
    e = exponent(part)
    part = part * jnp.exp2(12.0 - e)
    tail = columns(groups * height, e)
    for to, source in enumerate(order):
        out[to * height : (to + 1) * height, :features] = part[source * height : (source + 1) * height]
        out[to * height : (to + 1) * height, features:] = tail[source * height : (source + 1) * height]


def unit_kernel(got, out):
    copies, height, wide = out.shape
    features = wide - LANES
    full = jnp.zeros((height, features), F32)
    for source in range(got.shape[0]):
        full += got[source, :, :features] * jnp.exp2(got[source, :, features : features + 1] - 12.0)
    g = exponent(full)
    unit = full * jnp.exp2(-g)
    squares = jnp.sum(unit * unit, axis=-1, keepdims=True)
    unit = unit.astype(BF16)
    tail = columns(height, g, *pieces(squares)).astype(BF16)
    for copy in range(copies):
        out[copy, :, :features] = unit
        out[copy, :, features:] = tail


def score_kernel(got, index, other, out, held, sems):
    count, features = index.shape
    copies = [pltpu.make_async_copy(ref, held.at[i], sems.at[i]) for i, ref in enumerate((index, other))]
    for copy in copies:
        copy.start()
    out[:, 2 * count :] = got[:, features:].astype(F32)
    for i, copy in enumerate(copies):
        copy.wait()
        out[:, i * count : (i + 1) * count] = dot_t(got[:, :features], held[i]) * 8.0


def combine(got, wide, factor):
    sources = got.shape[0]
    tails = [got[i, :, wide:] for i in range(sources)]
    top = tails[0][:, :1]
    for tail in tails[1:]:
        top = jnp.maximum(top, tail[:, :1])
    total, squares = 0.0, 0.0
    for i, tail in enumerate(tails):
        scale = jnp.exp2(tail[:, :1] - top)
        total += got[i, :, :wide] * (scale * factor)
        squares += (tail[:, 1:2] + tail[:, 2:3] + tail[:, 3:4]) * (scale * scale)
    return total, squares, top


def middle_kernel(me, got, out):
    wide = got.shape[2] - LANES
    count = wide // 2
    total, squares, top = combine(got, wide, 0.25)
    tail = columns(total.shape[0], top, *pieces(squares))
    groups, _, height, _ = out.shape
    swapped = me[0] != 0
    own, other = total[:, :count], total[:, count:]
    halves = (jnp.where(swapped, other, own), jnp.where(swapped, own, other))
    for z in range(groups):
        for k, half in enumerate(halves):
            out[z, k, :, :count] = half[z * height : (z + 1) * height]
            out[z, k, :, count:] = tail[z * height : (z + 1) * height]


def last_kernel(got, out):
    wide = out.shape[1]
    total, squares, top = combine(got, wide, 0.5)
    out[...] = total / jnp.sqrt(squares + 1e-06 * jnp.exp2(-2.0 * jnp.maximum(top, -60.0)))


def call(kernel, spaces, shape, dtype, *args, **kwargs):
    return pl.pallas_call(
        kernel,
        out_shape=jax.ShapeDtypeStruct(shape, dtype),
        in_specs=[pl.BlockSpec(memory_space=space) for space in spaces],
        out_specs=pl.BlockSpec(memory_space=VMEM),
        compiler_params=pltpu.CompilerParams(vmem_limit_bytes=16 << 20),
        **kwargs,
    )(*args)


def swap(array):
    return lax.ppermute(array, "k", [(0, 1), (1, 0)])


def local(sizes, query, fisher, index):
    zh, x, zl, y, k = (sizes[a] for a in AXES)
    rows, pairs = zh * x, zl * y
    me = lax.axis_index("k").astype(jnp.int32).reshape(1)
    fisher_other = swap(fisher)
    index_other = swap(index)
    height, width = query.shape[0] // k, query.shape[1]
    features, count = fisher.shape[0], index.shape[0]
    batch = rows * height

    copies = jnp.broadcast_to(query[None], (rows,) + query.shape).reshape(-1, width)
    held = lax.all_to_all(copies, (*ROW, "k"), 0, 0, tiled=True).reshape(rows, k, height, width)

    order = tuple(z * x + i for i in range(x) for z in range(zh))
    sent = call(
        functools.partial(first_kernel, order), (SMEM, VMEM, VMEM, VMEM), (batch, features + LANES), F32,
        me, held, fisher, fisher_other,
    )
    got = lax.all_to_all(sent.astype(F16), PAIR, 0, 0, tiled=True).astype(F32)
    got = got.reshape(pairs, -1, features + LANES)

    sent = call(unit_kernel, (VMEM,), got.shape, BF16, got)
    got = lax.all_to_all(sent.reshape(batch, -1), PAIR, 0, 0, tiled=True)

    sent = call(
        score_kernel, (VMEM, pl.ANY, pl.ANY), (batch, 2 * count + LANES), F32, got, index, index_other,
        scratch_shapes=[VMEM((2, count, features), BF16), pltpu.SemaphoreType.DMA((2,))],
    )
    got = lax.all_to_all(sent.astype(F16), "x", 0, 0, tiled=True).astype(F32)
    got = got.reshape(x, zh * height, -1)

    sent = call(middle_kernel, (SMEM, VMEM), (zh, k, height, count + LANES), F32, me, got)
    sent = sent.reshape(zh * k * height, -1)
    got = lax.all_to_all(sent.astype(F16), ("zh", "k"), 0, 0, tiled=True).astype(F32)
    return call(last_kernel, (VMEM,), (k * height, count), F32, got.reshape(zh, k * height, -1))


def fine_mesh(mesh):
    rows, cols = mesh.devices.shape
    shape = (rows // 4, 4, 2, cols // 4, 2) if rows >= 16 else (2, rows // 2, 2, cols // 4, 2)
    return Mesh(mesh.devices.reshape(shape), AXES)


def solution(mesh):
    fine = fine_mesh(mesh)
    sizes = dict(fine.shape)
    row, col = ROW, (*PAIR, "k")
    placed = (P(row, col), P(row, col), P(col, row))
    return jax.shard_map(
        functools.partial(local, sizes), mesh=fine, in_specs=placed, out_specs=P(row, col), check_vma=False
    )
```

```python
import functools

import jax
import jax.numpy as jnp
from jax import lax
from jax.experimental import pallas as pl
from jax.experimental.pallas import tpu as pltpu
from jax.sharding import Mesh, PartitionSpec as P

F32, F16, BF16 = jnp.float32, jnp.float16, jnp.bfloat16
AXES = ("zh", "xh", "xl", "zl", "y", "k")
LANES = 128
VMEM, SMEM = pltpu.VMEM, pltpu.SMEM


def exponent(rows):
    top = jnp.max(jnp.abs(rows), axis=-1, keepdims=True)
    return jnp.clip(jnp.ceil(jnp.log2(jnp.maximum(top, 1e-30))), -100.0, 100.0)


def columns(height, *values):
    lane = lax.broadcasted_iota(jnp.int32, (height, LANES), 1)
    out = jnp.zeros((height, LANES), F32)
    for place, value in enumerate(values):
        out = jnp.where(lane == place, value, out)
    return out


def pieces(value):
    out = []
    for _ in range(3):
        out.append(value.astype(BF16).astype(F32))
        value = value - out[-1]
    return out


def dot_t(a, b):
    return lax.dot_general(a, b, (((1,), (1,)), ((), ())), preferred_element_type=F32)


def first_kernel(order, height, me, held, fisher, other, out):
    core = me[0]
    groups, _, rows, width = held.shape
    mine = held[:, core].reshape(groups * rows, width)
    theirs = held[:, 1 - core].reshape(groups * rows, width)
    part = dot_t(mine, fisher[...]) + dot_t(theirs, other[...])
    features = part.shape[1]
    e = exponent(part)
    part = part * jnp.exp2(12.0 - e)
    tail = columns(part.shape[0], e)
    for to, source in enumerate(order):
        out[to * height : (to + 1) * height, :features] = part[source * height : (source + 1) * height]
        out[to * height : (to + 1) * height, features:] = tail[source * height : (source + 1) * height]


def unit_kernel(got, out):
    blocks, sources, height, wide = got.shape
    features = wide - LANES
    full = []
    for block in range(blocks):
        total = jnp.zeros((height, features), F32)
        for i in range(sources):
            total += got[block, i, :, :features] * jnp.exp2(got[block, i, :, features : features + 1] - 12.0)
        full.append(total)
    full = jnp.concatenate(full, axis=1)
    g = exponent(full)
    unit = full * jnp.exp2(-g)
    squares = jnp.sum(unit * unit, axis=-1, keepdims=True)
    unit = unit.astype(BF16)
    tail = columns(height, g, *pieces(squares)).astype(BF16)
    for copy in range(out.shape[0]):
        out[copy, :, : blocks * features] = unit
        out[copy, :, blocks * features :] = tail


def score_kernel(me, got, own, across, core, core_across, out):
    count, features = own.shape
    mine = got[:, pl.ds(pl.multiple_of(me[1] * features, features), features)]
    theirs = got[:, pl.ds(pl.multiple_of((1 - me[1]) * features, features), features)]
    tail = got[:, 2 * features :].astype(F32)
    groups, _, height, _ = out.shape
    for k, here, there in ((me[0], own, across), (1 - me[0], core, core_across)):
        scores = (dot_t(mine, here[...]) + dot_t(theirs, there[...])) * 4.0
        for i in range(groups):
            out[i, k, :, :count] = scores[i * height : (i + 1) * height]
            out[i, k, :, count:] = tail[i * height : (i + 1) * height]


def last_kernel(got, out):
    wide = out.shape[1]
    tails = [got[i, :, wide:] for i in range(got.shape[0])]
    top = tails[0][:, :1]
    for tail in tails[1:]:
        top = jnp.maximum(top, tail[:, :1])
    total, squares = 0.0, 0.0
    for i, tail in enumerate(tails):
        scale = jnp.exp2(tail[:, :1] - top)
        total += got[i, :, :wide] * (scale * 0.25)
        squares += (tail[:, 1:2] + tail[:, 2:3] + tail[:, 3:4]) * (scale * scale)
    out[...] = total / jnp.sqrt(squares + 1e-06 * jnp.exp2(-2.0 * jnp.maximum(top, -60.0)))


def call(kernel, shape, dtype, *args):
    spaces = [SMEM if arg.dtype == jnp.int32 else VMEM for arg in args]
    return pl.pallas_call(
        kernel,
        out_shape=jax.ShapeDtypeStruct(shape, dtype),
        in_specs=[pl.BlockSpec(memory_space=space) for space in spaces],
        out_specs=pl.BlockSpec(memory_space=VMEM),
        compiler_params=pltpu.CompilerParams(vmem_limit_bytes=24 << 20),
    )(*args)


def swap(array, axis):
    return lax.ppermute(array, axis, [(0, 1), (1, 0)])


def local(sizes, query, fisher, index):
    zh, xh, xl, zl, y, k = (sizes[a] for a in AXES)
    x, pairs = xh * xl, zl * y
    me = jnp.stack([lax.axis_index("k"), lax.axis_index("xl")]).astype(jnp.int32)
    height, width = query.shape[0] // k, query.shape[1]
    features, count = fisher.shape[0], index.shape[0]
    batch = zh * x * height

    copies = jnp.broadcast_to(query[None], (zh,) + query.shape).reshape(-1, width)
    held = lax.all_to_all(copies, "zh", 0, 0, tiled=True).reshape(zh, k, height, width)
    fisher_core = swap(fisher, "k")
    copies = jnp.broadcast_to(held.transpose(1, 0, 2, 3)[None], (x, k, zh, height, width)).reshape(-1, width)
    held = lax.all_to_all(copies, ("xh", "xl", "k"), 0, 0, tiled=True).reshape(x, k, zh * height, width)

    index_across = swap(index, "xl")
    index_core = swap(index, "k")
    index_core_across = swap(index_across, "k")

    order = tuple((h * xl + i) * zh + z for i in range(xl) for z in range(zh) for h in range(xh))
    sent = call(
        functools.partial(first_kernel, order, height), (batch, features + LANES), F32, me, held, fisher, fisher_core
    )
    got = lax.all_to_all(sent.astype(F16), ("xl", "zl", "y"), 0, 0, tiled=True).astype(F32)
    got = got.reshape(xl, pairs, -1, features + LANES)

    sent = call(unit_kernel, (pairs, got.shape[2], xl * features + LANES), BF16, got)
    got = lax.all_to_all(sent.reshape(batch // xl, -1), ("zl", "y"), 0, 0, tiled=True)

    sent = call(
        score_kernel, (zh * xh, k, height, count + LANES), F32,
        me, got, index, index_across, index_core, index_core_across,
    )
    sent = sent.reshape(batch, -1)
    got = lax.all_to_all(sent.astype(F16), ("zh", "xh", "k"), 0, 0, tiled=True).astype(F32)
    return call(last_kernel, (k * height, count), F32, got.reshape(zh * xh, k * height, -1))


def fine_mesh(mesh):
    rows, cols = mesh.devices.shape
    return Mesh(mesh.devices.reshape(rows // 4, 2, 2, 2, cols // 4, 2), AXES)


def solution(mesh):
    fine = fine_mesh(mesh)
    sizes = dict(fine.shape)
    row, col = AXES[:3], AXES[3:]
    placed = (P(row, col), P(row, col), P(col, row))
    return jax.shard_map(
        functools.partial(local, sizes), mesh=fine, in_specs=placed, out_specs=P(row, col), check_vma=False
    )
```

```python
import functools

import jax
import jax.numpy as jnp
from jax import lax
from jax.experimental import pallas as pl
from jax.experimental.pallas import tpu as pltpu
from jax.sharding import Mesh, PartitionSpec as P

F32, F16, BF16 = jnp.float32, jnp.float16, jnp.bfloat16
AXES = ("zh", "xh", "xl", "zl", "y", "k")
LANES = 128
VMEM, SMEM = pltpu.VMEM, pltpu.SMEM


def exponent(rows):
    top = jnp.max(jnp.abs(rows), axis=-1, keepdims=True)
    return jnp.clip(jnp.ceil(jnp.log2(jnp.maximum(top, 1e-30))), -100.0, 100.0)


def columns(height, *values):
    lane = lax.broadcasted_iota(jnp.int32, (height, LANES), 1)
    out = jnp.zeros((height, LANES), F32)
    for place, value in enumerate(values):
        out = jnp.where(lane == place, value, out)
    return out


def pieces(value):
    out = []
    for _ in range(3):
        out.append(value.astype(BF16).astype(F32))
        value = value - out[-1]
    return out


def dot_t(a, b):
    return lax.dot_general(a, b, (((1,), (1,)), ((), ())), preferred_element_type=F32)


def first_kernel(order, height, me, held, fisher, other, out):
    core = me[0]
    groups, _, rows, width = held.shape
    mine = held[:, core].reshape(groups * rows, width)
    theirs = held[:, 1 - core].reshape(groups * rows, width)
    part = dot_t(mine, fisher[...]) + dot_t(theirs, other[...])
    features = part.shape[1]
    e = exponent(part)
    part = part * jnp.exp2(12.0 - e)
    tail = columns(part.shape[0], e)
    for to, source in enumerate(order):
        out[to * height : (to + 1) * height, :features] = part[source * height : (source + 1) * height]
        out[to * height : (to + 1) * height, features:] = tail[source * height : (source + 1) * height]


def unit_kernel(got, out):
    blocks, sources, height, wide = got.shape
    features = wide - LANES
    full = []
    for block in range(blocks):
        total = jnp.zeros((height, features), F32)
        for i in range(sources):
            total += got[block, i, :, :features] * jnp.exp2(got[block, i, :, features : features + 1] - 12.0)
        full.append(total)
    full = jnp.concatenate(full, axis=1)
    g = exponent(full)
    unit = full * jnp.exp2(-g)
    squares = jnp.sum(unit * unit, axis=-1, keepdims=True)
    unit = unit.astype(BF16)
    tail = columns(height, g, *pieces(squares)).astype(BF16)
    for copy in range(out.shape[0]):
        out[copy, :, : blocks * features] = unit
        out[copy, :, blocks * features :] = tail


def score_kernel(me, got, own, across, out, held, sems):
    count, features = own.shape
    copies = [pltpu.make_async_copy(ref, held.at[i], sems.at[i]) for i, ref in enumerate((own, across))]
    for copy in copies:
        copy.start()
    mine = got[:, pl.ds(pl.multiple_of(me[1] * features, features), features)]
    theirs = got[:, pl.ds(pl.multiple_of((1 - me[1]) * features, features), features)]
    copies[0].wait()
    scores = dot_t(mine, held[0])
    copies[1].wait()
    scores = (scores + dot_t(theirs, held[1])) * 4.0
    tail = got[:, 2 * features :].astype(F32)
    groups, _, height, _ = out.shape
    for i in range(groups):
        out[i, 0, :, :count] = scores[i * height : (i + 1) * height]
        out[i, 0, :, count:] = tail[i * height : (i + 1) * height]


def rest_kernel(me, got, own, across, done, out, held, sems):
    out[:, 1:] = done[...]
    score_kernel(me, got, own, across, out.at[:, 0:1], held, sems)


def combine(got, wide, factor):
    tails = [got[i, :, wide:] for i in range(got.shape[0])]
    top = tails[0][:, :1]
    for tail in tails[1:]:
        top = jnp.maximum(top, tail[:, :1])
    total, squares = 0.0, 0.0
    for i, tail in enumerate(tails):
        scale = jnp.exp2(tail[:, :1] - top)
        total += got[i, :, :wide] * (scale * factor)
        squares += (tail[:, 1:2] + tail[:, 2:3] + tail[:, 3:4]) * (scale * scale)
    return total, squares, top


def middle_kernel(got, out):
    wide = got.shape[2] - LANES
    total, squares, top = combine(got, wide, 0.5)
    out[:, :wide] = total
    out[:, wide:] = columns(total.shape[0], top, *pieces(squares))


def last_kernel(me, got, out):
    total, squares, top = combine(got, out.shape[2], 0.5)
    total = total / jnp.sqrt(squares + 1e-06 * jnp.exp2(-2.0 * jnp.maximum(top, -60.0)))
    height = out.shape[1]
    out[1 - me[0]] = total[:height]
    out[me[0]] = total[height:]


def call(kernel, shape, dtype, *args, spaces=None, **kwargs):
    spaces = spaces or [SMEM if arg.dtype == jnp.int32 else VMEM for arg in args]
    return pl.pallas_call(
        kernel,
        out_shape=jax.ShapeDtypeStruct(shape, dtype),
        in_specs=[pl.BlockSpec(memory_space=space) for space in spaces],
        out_specs=pl.BlockSpec(memory_space=VMEM),
        compiler_params=pltpu.CompilerParams(vmem_limit_bytes=24 << 20),
        **kwargs,
    )(*args)


def swap(array, axis):
    return lax.ppermute(array, axis, [(0, 1), (1, 0)])


def local(sizes, query, fisher, index):
    zh, xh, xl, zl, y, k = (sizes[a] for a in AXES)
    x, pairs = xh * xl, zl * y
    me = jnp.stack([lax.axis_index("k"), lax.axis_index("xl")]).astype(jnp.int32)
    height, width = query.shape[0] // k, query.shape[1]
    features, count = fisher.shape[0], index.shape[0]
    batch = zh * x * height

    copies = jnp.broadcast_to(query[None], (zh,) + query.shape).reshape(-1, width)
    held = lax.all_to_all(copies, "zh", 0, 0, tiled=True).reshape(zh, k, height, width)
    fisher_core = swap(fisher, "k")
    copies = jnp.broadcast_to(held.transpose(1, 0, 2, 3)[None], (x, k, zh, height, width)).reshape(-1, width)
    held = lax.all_to_all(copies, ("xh", "xl", "k"), 0, 0, tiled=True).reshape(x, k, zh * height, width)

    order = tuple((h * xl + i) * zh + z for i in range(xl) for h in range(xh) for z in range(zh))
    sent = call(
        functools.partial(first_kernel, order, height), (batch, features + LANES), F32, me, held, fisher, fisher_core
    )
    index_across = swap(index, "xl")
    got = lax.all_to_all(sent.astype(F16), ("xl", "zl", "y"), 0, 0, tiled=True).astype(F32)
    got = got.reshape(xl, pairs, -1, features + LANES)

    sent = call(unit_kernel, (pairs, got.shape[2], xl * features + LANES), BF16, got)
    got = lax.all_to_all(sent.reshape(batch // xl, -1), ("zl", "y"), 0, 0, tiled=True)

    blocks = zh * xh
    spaces = (SMEM, VMEM) + (pl.ANY,) * 2
    scratch = [VMEM((2, count, features), BF16), pltpu.SemaphoreType.DMA((2,))]
    cost = pl.CostEstimate(
        flops=4 * blocks * height * count * features, bytes_accessed=4 * count * features, transcendentals=0
    )
    more = dict(scratch_shapes=scratch, cost_estimate=cost)
    others = swap(got, "k")
    shape = (blocks, 1, height, count + LANES)
    done = call(score_kernel, shape, F32, me, got, index, index_across, spaces=spaces, **more)
    shape = (blocks, k, height, count + LANES)
    sent = call(rest_kernel, shape, F32, me, others, index, index_across, done, spaces=spaces + (VMEM,), **more)
    sent = sent.reshape(batch, -1)
    got = lax.all_to_all(sent.astype(F16), "xh", 0, 0, tiled=True).astype(F32).reshape(xh, zh * k * height, -1)

    sent = call(middle_kernel, got.shape[1:], F32, got)
    got = lax.all_to_all(sent.astype(F16), "zh", 0, 0, tiled=True).astype(F32).reshape(zh, k * height, -1)
    return call(last_kernel, (k, height, count), F32, me, got).reshape(k * height, count)


def fine_mesh(mesh):
    rows, cols = mesh.devices.shape
    return Mesh(mesh.devices.reshape(rows // 4, 2, 2, 2, cols // 4, 2), AXES)


def solution(mesh):
    fine = fine_mesh(mesh)
    sizes = dict(fine.shape)
    row, col = AXES[:3], AXES[3:]
    placed = (P(row, col), P(row, col), P(col, row))
    return jax.shard_map(
        functools.partial(local, sizes), mesh=fine, in_specs=placed, out_specs=P(row, col), check_vma=False
    )
```

```python
import functools

import jax
import jax.numpy as jnp
from jax import lax
from jax.experimental import pallas as pl
from jax.experimental.pallas import tpu as pltpu
from jax.sharding import Mesh, PartitionSpec as P

F32, F16, BF16 = jnp.float32, jnp.float16, jnp.bfloat16
AXES = ("zh", "x", "zl", "y", "k")
ROW = ("zh", "x")
PAIR = ("zl", "y")
LANES = 128
VMEM, SMEM = pltpu.VMEM, pltpu.SMEM


def exponent(rows):
    top = jnp.max(jnp.abs(rows), axis=-1, keepdims=True)
    return jnp.clip(jnp.ceil(jnp.log2(jnp.maximum(top, 1e-30))), -100.0, 100.0)


def columns(height, *values):
    lane = lax.broadcasted_iota(jnp.int32, (height, LANES), 1)
    out = jnp.zeros((height, LANES), F32)
    for place, value in enumerate(values):
        out = jnp.where(lane == place, value, out)
    return out


def pieces(value):
    out = []
    for _ in range(3):
        out.append(value.astype(BF16).astype(F32))
        value = value - out[-1]
    return out


def dot_t(a, b):
    return lax.dot_general(a, b, (((1,), (1,)), ((), ())), preferred_element_type=F32)


def first_kernel(order, me, held, fisher, other, out):
    core = me[0]
    groups, _, height, width = held.shape
    mine = held[:, core].reshape(groups * height, width)
    theirs = held[:, 1 - core].reshape(groups * height, width)
    part = dot_t(mine, fisher[...]) + dot_t(theirs, other[...])
    features = part.shape[1]
    e = exponent(part)
    part = part * jnp.exp2(12.0 - e)
    tail = columns(groups * height, e)
    for to, source in enumerate(order):
        out[to * height : (to + 1) * height, :features] = part[source * height : (source + 1) * height]
        out[to * height : (to + 1) * height, features:] = tail[source * height : (source + 1) * height]


def unit_kernel(got, out):
    copies, height, wide = out.shape
    features = wide - LANES
    full = jnp.zeros((height, features), F32)
    for source in range(got.shape[0]):
        full += got[source, :, :features] * jnp.exp2(got[source, :, features : features + 1] - 12.0)
    g = exponent(full)
    unit = full * jnp.exp2(-g)
    squares = jnp.sum(unit * unit, axis=-1, keepdims=True)
    unit = unit.astype(BF16)
    tail = columns(height, g, *pieces(squares)).astype(BF16)
    for copy in range(copies):
        out[copy, :, :features] = unit
        out[copy, :, features:] = tail


def score_kernel(got, index, other, out, held, sem):
    count, features = index.shape
    copy = pltpu.make_async_copy(other, held, sem)
    copy.start()
    out[:, 2 * count :] = got[:, features:].astype(F32)
    out[:, :count] = dot_t(got[:, :features], index[...]) * 8.0
    copy.wait()
    out[:, count : 2 * count] = dot_t(got[:, :features], held[...]) * 8.0


def combine(got, wide, factor):
    sources = got.shape[0]
    tails = [got[i, :, wide:] for i in range(sources)]
    top = tails[0][:, :1]
    for tail in tails[1:]:
        top = jnp.maximum(top, tail[:, :1])
    total, squares = 0.0, 0.0
    for i, tail in enumerate(tails):
        scale = jnp.exp2(tail[:, :1] - top)
        total += got[i, :, :wide] * (scale * factor)
        squares += (tail[:, 1:2] + tail[:, 2:3] + tail[:, 3:4]) * (scale * scale)
    return total, squares, top


def middle_kernel(me, got, out):
    wide = got.shape[2] - LANES
    count = wide // 2
    total, squares, top = combine(got, wide, 0.25)
    tail = columns(total.shape[0], top, *pieces(squares))
    groups, _, height, _ = out.shape
    swapped = me[0] != 0
    own, other = total[:, :count], total[:, count:]
    halves = (jnp.where(swapped, other, own), jnp.where(swapped, own, other))
    for z in range(groups):
        for k, half in enumerate(halves):
            out[z, k, :, :count] = half[z * height : (z + 1) * height]
            out[z, k, :, count:] = tail[z * height : (z + 1) * height]


def last_kernel(got, out):
    wide = out.shape[1]
    total, squares, top = combine(got, wide, 0.5)
    out[...] = total / jnp.sqrt(squares + 1e-06 * jnp.exp2(-2.0 * jnp.maximum(top, -60.0)))


def call(kernel, spaces, shape, dtype, *args, **kwargs):
    return pl.pallas_call(
        kernel,
        out_shape=jax.ShapeDtypeStruct(shape, dtype),
        in_specs=[pl.BlockSpec(memory_space=space) for space in spaces],
        out_specs=pl.BlockSpec(memory_space=VMEM),
        compiler_params=pltpu.CompilerParams(vmem_limit_bytes=16 << 20),
        **kwargs,
    )(*args)


def swap(array):
    return lax.ppermute(array, "k", [(0, 1), (1, 0)])


def local(sizes, query, fisher, index):
    zh, x, zl, y, k = (sizes[a] for a in AXES)
    rows, pairs = zh * x, zl * y
    me = lax.axis_index("k").astype(jnp.int32).reshape(1)
    fisher_other = swap(fisher)
    index_other = swap(index)
    height, width = query.shape[0] // k, query.shape[1]
    features, count = fisher.shape[0], index.shape[0]
    batch = rows * height

    copies = jnp.broadcast_to(query[None], (rows,) + query.shape).reshape(-1, width)
    held = lax.all_to_all(copies, (*ROW, "k"), 0, 0, tiled=True)
    held = held.reshape(rows, k, height, width)

    order = tuple(z * x + i for i in range(x) for z in range(zh))
    sent = call(
        functools.partial(first_kernel, order), (SMEM, VMEM, VMEM, VMEM), (batch, features + LANES), F32,
        me, held, fisher, fisher_other,
    )
    sent = sent.astype(F16)
    got = lax.all_to_all(sent, PAIR, 0, 0, tiled=True)
    got = got.astype(F32).reshape(pairs, -1, features + LANES)

    sent = call(unit_kernel, (VMEM,), got.shape, BF16, got)
    got = lax.all_to_all(sent.reshape(batch, -1), PAIR, 0, 0, tiled=True)

    sent = call(
        score_kernel, (VMEM, VMEM, pl.ANY), (batch, 2 * count + LANES), F32, got, index, index_other,
        scratch_shapes=[VMEM((count, features), BF16), pltpu.SemaphoreType.DMA],
    )
    got = lax.all_to_all(sent.astype(F16), "x", 0, 0, tiled=True).astype(F32)
    got = got.reshape(x, zh * height, -1)

    sent = call(middle_kernel, (SMEM, VMEM), (zh, k, height, count + LANES), F32, me, got)
    sent = sent.reshape(zh * k * height, -1)
    got = lax.all_to_all(sent.astype(F16), ("zh", "k"), 0, 0, tiled=True).astype(F32)
    return call(last_kernel, (VMEM,), (k * height, count), F32, got.reshape(zh, k * height, -1))


def fine_mesh(mesh):
    rows, cols = mesh.devices.shape
    shape = (rows // 4, 4, 2, cols // 4, 2) if rows >= 16 else (2, rows // 2, 2, cols // 4, 2)
    return Mesh(mesh.devices.reshape(shape), AXES)


def solution(mesh):
    fine = fine_mesh(mesh)
    sizes = dict(fine.shape)
    row, col = ROW, (*PAIR, "k")
    placed = (P(row, col), P(row, col), P(col, row))
    return jax.shard_map(
        functools.partial(local, sizes), mesh=fine, in_specs=placed, out_specs=P(row, col), check_vma=False
    )
```

```python
import functools

import jax
import jax.numpy as jnp
from jax import lax
from jax.experimental import pallas as pl
from jax.experimental.pallas import tpu as pltpu
from jax.sharding import Mesh, PartitionSpec as P

F32, F16, BF16 = jnp.float32, jnp.float16, jnp.bfloat16
AXES = ("zh", "x", "zl", "y", "k")
ROW = ("zh", "x")
PAIR = ("zl", "y")
LANES = 128
TAIL = 8
VMEM, SMEM = pltpu.VMEM, pltpu.SMEM


def exponent(rows):
    top = jnp.max(jnp.abs(rows), axis=-1, keepdims=True)
    return jnp.clip(jnp.ceil(jnp.log2(jnp.maximum(top, 1e-30))), -100.0, 100.0)


def diagonal(height):
    return lax.broadcasted_iota(jnp.int32, (height, LANES), 0) == lax.broadcasted_iota(jnp.int32, (height, LANES), 1)


def across(*columns):
    here = diagonal(columns[0].shape[0])
    row = lax.broadcasted_iota(jnp.int32, (TAIL, LANES), 0)
    out = jnp.zeros((TAIL, LANES), F32)
    for place, column in enumerate(columns):
        out = jnp.where(row == place, jnp.sum(jnp.where(here, column, 0.0), axis=0, keepdims=True), out)
    return out


def down(row, height):
    return jnp.sum(jnp.where(diagonal(height), row, 0.0), axis=1, keepdims=True)


def pieces(value):
    out = []
    for _ in range(3):
        out.append(value.astype(BF16).astype(F32))
        value = value - out[-1]
    return out


def dot_t(a, b):
    return lax.dot_general(a, b, (((1,), (1,)), ((), ())), preferred_element_type=F32)


def copy_kernel(query, out):
    for i in range(out.shape[0]):
        out[i] = query[...]


def first_kernel(order, me, held, fisher, other, out):
    core = me[0]
    groups, _, height, width = held.shape
    mine = held[:, core].reshape(groups * height, width)
    theirs = held[:, 1 - core].reshape(groups * height, width)
    part = dot_t(mine, fisher[...]) + dot_t(theirs, other[...])
    tiles = part.shape[1] // LANES
    e = exponent(part)
    part = part * jnp.exp2(12.0 - e)
    for to, source in enumerate(order):
        rows = slice(source * height, (source + 1) * height)
        for c in range(tiles):
            out[to, c * height : (c + 1) * height] = part[rows, c * LANES : (c + 1) * LANES]
        out[to, tiles * height :] = across(e[rows])


def unit_kernel(height, got, out):
    tiles = (out.shape[1] - TAIL) // height
    full = [jnp.zeros((height, LANES), F32)] * tiles
    for i in range(got.shape[0]):
        scale = jnp.exp2(down(got[i, tiles * height : tiles * height + 1], height) - 12.0)
        full = [full[c] + got[i, c * height : (c + 1) * height] * scale for c in range(tiles)]
    full = jnp.concatenate(full, axis=1)
    g = exponent(full)
    unit = full * jnp.exp2(-g)
    squares = jnp.sum(unit * unit, axis=-1, keepdims=True)
    unit = unit.astype(BF16)
    tail = across(g, *pieces(squares)).astype(BF16)
    for copy in range(out.shape[0]):
        for c in range(tiles):
            out[copy, c * height : (c + 1) * height] = unit[:, c * LANES : (c + 1) * LANES]
        out[copy, tiles * height :] = tail


def score_kernel(height, got, index, other, out, held, sem):
    count, features = index.shape
    copy = pltpu.make_async_copy(other, held, sem)
    copy.start()
    sources, tiles = got.shape[0], features // LANES
    unit = jnp.concatenate(
        [got[:, c * height : (c + 1) * height].reshape(sources * height, LANES) for c in range(tiles)], axis=1
    )
    tails = got[:, tiles * height :].astype(F32)
    chunks = out.shape[0]
    per = sources // chunks
    rows = per * height
    tiles = count // LANES
    for i in range(chunks):
        tail = tails[i * per]
        for z in range(1, per):
            tail += pltpu.roll(tails[i * per + z], z * height, 1)
        out[i, 2 * tiles * rows :] = tail

    def put(block, scores):
        for i in range(chunks):
            for c in range(tiles):
                at = (block * tiles + c) * rows
                out[i, at : at + rows] = scores[i * rows : (i + 1) * rows, c * LANES : (c + 1) * LANES]

    put(0, dot_t(unit, index[...]) * 8.0)
    copy.wait()
    put(1, dot_t(unit, held[...]) * 8.0)


def combine(tiles, height, factor, got):
    tails = [[down(block[tiles * height + t : tiles * height + t + 1], height) for t in range(4)] for block in got]
    top = tails[0][0]
    for tail in tails[1:]:
        top = jnp.maximum(top, tail[0])
    total, squares = [0.0] * tiles, 0.0
    for block, (g, *parts) in zip(got, tails):
        scale = jnp.exp2(g - top)
        squares += sum(parts) * (scale * scale)
        scale = scale * factor
        total = [total[c] + block[c * height : (c + 1) * height] * scale for c in range(tiles)]
    return total, squares, top


def middle_kernel(height, me, got, out):
    groups = out.shape[0]
    rows = groups * height
    tiles = (out.shape[2] - TAIL) // height
    total, squares, top = combine(2 * tiles, rows, 0.25, [got.at[i] for i in range(got.shape[0])])
    values = (top, *pieces(squares))
    for z in range(groups):
        here = slice(z * height, (z + 1) * height)
        tail = across(*(value[here] for value in values))
        for block, k in enumerate((me[0], 1 - me[0])):
            for c in range(tiles):
                out[z, k, c * height : (c + 1) * height] = total[block * tiles + c][here]
            out[z, k, tiles * height :] = tail


def last_kernel(height, got, out):
    tiles = out.shape[1] // LANES
    for k in range(got.shape[1]):
        total, squares, top = combine(tiles, height, 0.5, [got.at[i, k] for i in range(got.shape[0])])
        norm = jnp.sqrt(squares + 1e-06 * jnp.exp2(-2.0 * jnp.maximum(top, -60.0)))
        for c in range(tiles):
            out[k * height : (k + 1) * height, c * LANES : (c + 1) * LANES] = total[c] / norm


def call(kernel, spaces, shape, dtype, *args, **kwargs):
    return pl.pallas_call(
        kernel,
        out_shape=jax.ShapeDtypeStruct(shape, dtype),
        in_specs=[pl.BlockSpec(memory_space=space) for space in spaces],
        out_specs=pl.BlockSpec(memory_space=VMEM),
        compiler_params=pltpu.CompilerParams(vmem_limit_bytes=16 << 20),
        **kwargs,
    )(*args)


def swap(array):
    return lax.ppermute(array, "k", [(0, 1), (1, 0)])


def local(sizes, query, fisher, index):
    zh, x, zl, y, k = (sizes[a] for a in AXES)
    rows, pairs = zh * x, zl * y
    me = lax.axis_index("k").astype(jnp.int32).reshape(1)
    fisher_other = swap(fisher)
    index_other = swap(index)
    height, width = query.shape[0] // k, query.shape[1]
    features, count = fisher.shape[0], index.shape[0]
    deep = features // LANES * height + TAIL
    wide = 2 * (count // LANES) * zh * height + TAIL
    short = count // LANES * height + TAIL

    def exchange(sent, axes, shape):
        return lax.all_to_all(sent.reshape(-1, LANES), axes, 0, 0, tiled=True).reshape(shape)

    copies = call(copy_kernel, (VMEM,), (rows,) + query.shape, BF16, query).reshape(-1, width)
    held = lax.all_to_all(copies, (*ROW, "k"), 0, 0, tiled=True)
    held = held.reshape(rows, k, height, width)

    order = tuple(z * x + i for i in range(x) for z in range(zh))
    sent = call(
        functools.partial(first_kernel, order), (SMEM, VMEM, VMEM, VMEM), (pairs, deep, LANES), F32,
        me, held, fisher, fisher_other,
    )
    got = exchange(sent.astype(F16), PAIR, (pairs, deep, LANES)).astype(F32)

    sent = call(functools.partial(unit_kernel, height), (VMEM,), got.shape, BF16, got)
    got = exchange(sent, PAIR, got.shape)

    sent = call(
        functools.partial(score_kernel, height), (VMEM, VMEM, pl.ANY), (x, wide, LANES), F32, got, index, index_other,
        scratch_shapes=[VMEM((count, features), BF16), pltpu.SemaphoreType.DMA],
    )
    got = exchange(sent.astype(F16), "x", sent.shape).astype(F32)

    sent = call(functools.partial(middle_kernel, height), (SMEM, VMEM), (zh, k, short, LANES), F32, me, got)
    got = exchange(sent.astype(F16), ("zh", "k"), sent.shape).astype(F32)
    return call(functools.partial(last_kernel, height), (VMEM,), (k * height, count), F32, got)


def fine_mesh(mesh):
    rows, cols = mesh.devices.shape
    shape = (rows // 4, 4, 2, cols // 4, 2) if rows >= 16 else (2, rows // 2, 2, cols // 4, 2)
    return Mesh(mesh.devices.reshape(shape), AXES)


def solution(mesh):
    fine = fine_mesh(mesh)
    sizes = dict(fine.shape)
    row, col = ROW, (*PAIR, "k")
    placed = (P(row, col), P(row, col), P(col, row))
    return jax.shard_map(
        functools.partial(local, sizes), mesh=fine, in_specs=placed, out_specs=P(row, col), check_vma=False
    )
```

```python
import functools

import jax
import jax.numpy as jnp
from jax import lax
from jax.experimental import pallas as pl
from jax.experimental.pallas import tpu as pltpu
from jax.sharding import Mesh, PartitionSpec as P

F32, F16, BF16 = jnp.float32, jnp.float16, jnp.bfloat16
AXES = ("zh", "x", "zl", "y", "k")
ROW = ("zh", "x")
PAIR = ("zl", "y")
LANES = 128
TAIL = 8
VMEM, SMEM = pltpu.VMEM, pltpu.SMEM


def exponent(rows):
    top = jnp.max(jnp.abs(rows), axis=-1, keepdims=True)
    return jnp.clip(jnp.ceil(jnp.log2(jnp.maximum(top, 1e-30))), -100.0, 100.0)


def diagonal(height):
    return lax.broadcasted_iota(jnp.int32, (height, LANES), 0) == lax.broadcasted_iota(jnp.int32, (height, LANES), 1)


def across(*columns):
    here = diagonal(columns[0].shape[0])
    row = lax.broadcasted_iota(jnp.int32, (TAIL, LANES), 0)
    out = jnp.zeros((TAIL, LANES), F32)
    for place, column in enumerate(columns):
        out = jnp.where(row == place, jnp.sum(jnp.where(here, column, 0.0), axis=0, keepdims=True), out)
    return out


def down(row, height):
    return jnp.sum(jnp.where(diagonal(height), row, 0.0), axis=1, keepdims=True)


def pieces(value):
    out = []
    for _ in range(3):
        out.append(value.astype(BF16).astype(F32))
        value = value - out[-1]
    return out


def dot_t(a, b):
    return lax.dot_general(a, b, (((1,), (1,)), ((), ())), preferred_element_type=F32)


def copy_kernel(me, mine, theirs, out):
    height = out.shape[2]
    rows = pl.ds(pl.multiple_of(me[0] * height, height), height)
    blocks = mine[rows], theirs[rows]
    for i in range(out.shape[0]):
        for k, block in enumerate(blocks):
            out[i, k] = block


def first_kernel(held, fisher, other, out):
    groups, _, height, width = held.shape
    mine = held[:, 0].reshape(groups * height, width)
    theirs = held[:, 1].reshape(groups * height, width)
    part = dot_t(mine, fisher[...]) + dot_t(theirs, other[...])
    tiles = part.shape[1] // LANES
    e = exponent(part)
    part = part * jnp.exp2(12.0 - e)
    for i in range(groups):
        rows = slice(i * height, (i + 1) * height)
        for c in range(tiles):
            out[i, c * height : (c + 1) * height] = part[rows, c * LANES : (c + 1) * LANES]
        out[i, tiles * height :] = across(e[rows])


def unit_kernel(height, got, out):
    tiles = (out.shape[1] - TAIL) // height
    full = [jnp.zeros((height, LANES), F32)] * tiles
    for i in range(got.shape[0]):
        scale = jnp.exp2(down(got[i, tiles * height : tiles * height + 1], height) - 12.0)
        full = [full[c] + got[i, c * height : (c + 1) * height] * scale for c in range(tiles)]
    full = jnp.concatenate(full, axis=1)
    g = exponent(full)
    unit = full * jnp.exp2(-g)
    squares = jnp.sum(unit * unit, axis=-1, keepdims=True)
    unit = unit.astype(BF16)
    tail = across(g, *pieces(squares)).astype(BF16)
    for copy in range(out.shape[0]):
        for c in range(tiles):
            out[copy, c * height : (c + 1) * height] = unit[:, c * LANES : (c + 1) * LANES]
        out[copy, tiles * height :] = tail


def score_kernel(height, got, index, other, out, held, sem):
    count, features = index.shape
    copy = pltpu.make_async_copy(other, held, sem)
    copy.start()
    sources, tiles = got.shape[0], features // LANES
    unit = jnp.concatenate(
        [got[:, c * height : (c + 1) * height].reshape(sources * height, LANES) for c in range(tiles)], axis=1
    )
    tails = got[:, tiles * height :].astype(F32)
    chunks = out.shape[0]
    per = sources // chunks
    rows = per * height
    tiles = count // LANES
    for i in range(chunks):
        tail = tails[i * per]
        for z in range(1, per):
            tail += pltpu.roll(tails[i * per + z], z * height, 1)
        out[i, 2 * tiles * rows :] = tail

    def put(block, scores):
        for i in range(chunks):
            for c in range(tiles):
                at = (block * tiles + c) * rows
                out[i, at : at + rows] = scores[i * rows : (i + 1) * rows, c * LANES : (c + 1) * LANES]

    put(0, dot_t(unit, index[...]) * 8.0)
    copy.wait()
    put(1, dot_t(unit, held[...]) * 8.0)


def combine(tiles, height, factor, got):
    tails = [[down(block[tiles * height + t : tiles * height + t + 1], height) for t in range(4)] for block in got]
    top = tails[0][0]
    for tail in tails[1:]:
        top = jnp.maximum(top, tail[0])
    total, squares = [0.0] * tiles, 0.0
    for block, (g, *parts) in zip(got, tails):
        scale = jnp.exp2(g - top)
        squares += sum(parts) * (scale * scale)
        scale = scale * factor
        total = [total[c] + block[c * height : (c + 1) * height] * scale for c in range(tiles)]
    return total, squares, top


def middle_kernel(height, me, got, out):
    groups = out.shape[0]
    rows = groups * height
    tiles = (out.shape[2] - TAIL) // height
    total, squares, top = combine(2 * tiles, rows, 0.25, [got.at[i] for i in range(got.shape[0])])
    values = (top, *pieces(squares))
    for z in range(groups):
        here = slice(z * height, (z + 1) * height)
        tail = across(*(value[here] for value in values))
        for block, k in enumerate((me[0], 1 - me[0])):
            for c in range(tiles):
                out[z, k, c * height : (c + 1) * height] = total[block * tiles + c][here]
            out[z, k, tiles * height :] = tail


def last_kernel(height, got, out):
    tiles = out.shape[1] // LANES
    for k in range(got.shape[1]):
        total, squares, top = combine(tiles, height, 0.5, [got.at[i, k] for i in range(got.shape[0])])
        norm = jnp.sqrt(squares + 1e-06 * jnp.exp2(-2.0 * jnp.maximum(top, -60.0)))
        for c in range(tiles):
            out[k * height : (k + 1) * height, c * LANES : (c + 1) * LANES] = total[c] / norm


def call(kernel, spaces, shape, dtype, *args, **kwargs):
    return pl.pallas_call(
        kernel,
        out_shape=jax.ShapeDtypeStruct(shape, dtype),
        in_specs=[pl.BlockSpec(memory_space=space) for space in spaces],
        out_specs=pl.BlockSpec(memory_space=VMEM),
        compiler_params=pltpu.CompilerParams(vmem_limit_bytes=16 << 20),
        **kwargs,
    )(*args)


def swap(array):
    return lax.ppermute(array, "k", [(0, 1), (1, 0)])


def local(sizes, query, fisher, index):
    zh, x, zl, y, k = (sizes[a] for a in AXES)
    rows, pairs = zh * x, zl * y
    me = lax.axis_index("k").astype(jnp.int32).reshape(1)
    fisher_other = swap(fisher)
    index_other = swap(index)
    height, width = query.shape[0] // k, query.shape[1]
    features, count = fisher.shape[0], index.shape[0]
    deep = features // LANES * height + TAIL
    wide = 2 * (count // LANES) * zh * height + TAIL
    short = count // LANES * height + TAIL

    def exchange(sent, axes, shape):
        return lax.all_to_all(sent.reshape(-1, LANES), axes, 0, 0, tiled=True).reshape(shape)

    copies = call(copy_kernel, (SMEM, VMEM, VMEM), (rows, k, height, width), BF16, me, query, swap(query))
    held = lax.all_to_all(copies.reshape(-1, width), ("x", "zh"), 0, 0, tiled=True)
    held = held.reshape(rows, k, height, width)

    sent = call(first_kernel, (VMEM, VMEM, VMEM), (pairs, deep, LANES), F32, held, fisher, fisher_other)
    got = exchange(sent.astype(F16), PAIR, (pairs, deep, LANES)).astype(F32)

    sent = call(functools.partial(unit_kernel, height), (VMEM,), got.shape, BF16, got)
    got = exchange(sent, PAIR, got.shape)

    sent = call(
        functools.partial(score_kernel, height), (VMEM, VMEM, pl.ANY), (x, wide, LANES), F32, got, index, index_other,
        scratch_shapes=[VMEM((count, features), BF16), pltpu.SemaphoreType.DMA],
    )
    got = exchange(sent.astype(F16), "x", sent.shape).astype(F32)

    sent = call(functools.partial(middle_kernel, height), (SMEM, VMEM), (zh, k, short, LANES), F32, me, got)
    got = exchange(sent.astype(F16), ("zh", "k"), sent.shape).astype(F32)
    return call(functools.partial(last_kernel, height), (VMEM,), (k * height, count), F32, got)


def fine_mesh(mesh):
    rows, cols = mesh.devices.shape
    shape = (rows // 4, 4, 2, cols // 4, 2) if rows >= 16 else (2, rows // 2, 2, cols // 4, 2)
    return Mesh(mesh.devices.reshape(shape), AXES)


def solution(mesh):
    fine = fine_mesh(mesh)
    sizes = dict(fine.shape)
    row, col = ROW, (*PAIR, "k")
    placed = (P(row, col), P(row, col), P(col, row))
    return jax.shard_map(
        functools.partial(local, sizes), mesh=fine, in_specs=placed, out_specs=P(row, col), check_vma=False
    )
```

```python
import functools

import jax
import jax.numpy as jnp
from jax import lax
from jax.experimental import pallas as pl
from jax.experimental.pallas import tpu as pltpu
from jax.sharding import Mesh, PartitionSpec as P

F32, F16, BF16 = jnp.float32, jnp.float16, jnp.bfloat16
AXES = ("zh", "x", "zl", "y", "k")
ROW = ("zh", "x")
PAIR = ("zl", "y")
LANES = 128
TAIL = 8
VMEM, SMEM = pltpu.VMEM, pltpu.SMEM


def exponent(rows):
    top = jnp.max(jnp.abs(rows), axis=-1, keepdims=True)
    return jnp.clip(jnp.ceil(jnp.log2(jnp.maximum(top, 1e-30))), -100.0, 100.0)


def diagonal(height):
    return lax.broadcasted_iota(jnp.int32, (height, LANES), 0) == lax.broadcasted_iota(jnp.int32, (height, LANES), 1)


def across(*columns):
    here = diagonal(columns[0].shape[0])
    row = lax.broadcasted_iota(jnp.int32, (TAIL, LANES), 0)
    out = jnp.zeros((TAIL, LANES), F32)
    for place, column in enumerate(columns):
        out = jnp.where(row == place, jnp.sum(jnp.where(here, column, 0.0), axis=0, keepdims=True), out)
    return out


def down(row, height):
    return jnp.sum(jnp.where(diagonal(height), row, 0.0), axis=1, keepdims=True)


def pieces(value):
    out = []
    for _ in range(3):
        out.append(value.astype(BF16).astype(F32))
        value = value - out[-1]
    return out


def dot_t(a, b):
    return lax.dot_general(a, b, (((1,), (1,)), ((), ())), preferred_element_type=F32)


def copy_kernel(query, out):
    for i in range(out.shape[0]):
        out[i] = query[...]


def first_kernel(me, held, fisher, other, out):
    core = me[0]
    groups, _, height, width = held.shape
    mine = held[:, core].reshape(groups * height, width)
    theirs = held[:, 1 - core].reshape(groups * height, width)
    part = dot_t(mine, fisher[...]) + dot_t(theirs, other[...])
    tiles = part.shape[1] // LANES
    e = exponent(part)
    part = part * jnp.exp2(12.0 - e)
    for i in range(groups):
        rows = slice(i * height, (i + 1) * height)
        for c in range(tiles):
            out[i, c * height : (c + 1) * height] = part[rows, c * LANES : (c + 1) * LANES]
        out[i, tiles * height :] = across(e[rows])


def unit_kernel(height, got, out):
    tiles = (out.shape[1] - TAIL) // height
    full = [jnp.zeros((height, LANES), F32)] * tiles
    for i in range(got.shape[0]):
        scale = jnp.exp2(down(got[i, tiles * height : tiles * height + 1], height) - 12.0)
        full = [full[c] + got[i, c * height : (c + 1) * height] * scale for c in range(tiles)]
    full = jnp.concatenate(full, axis=1)
    g = exponent(full)
    unit = full * jnp.exp2(-g)
    squares = jnp.sum(unit * unit, axis=-1, keepdims=True)
    unit = unit.astype(BF16)
    tail = across(g, *pieces(squares)).astype(BF16)
    for copy in range(out.shape[0]):
        for c in range(tiles):
            out[copy, c * height : (c + 1) * height] = unit[:, c * LANES : (c + 1) * LANES]
        out[copy, tiles * height :] = tail


def unit_scores(height, got, index):
    sources, tiles = got.shape[0], index.shape[1] // LANES
    unit = jnp.concatenate(
        [got[:, c * height : (c + 1) * height].reshape(sources * height, LANES) for c in range(tiles)], axis=1
    )
    return dot_t(unit, index[...]) * 8.0, got[:, tiles * height :].astype(F32)


def score_kernel(height, got, index, out):
    scores, tails = unit_scores(height, got, index)
    tiles = index.shape[0] // LANES
    for i in range(out.shape[0]):
        for c in range(tiles):
            rows = scores[i * height : (i + 1) * height, c * LANES : (c + 1) * LANES]
            out[i, c * height : (c + 1) * height] = rows
        out[i, tiles * height :] = tails[i]


def rest_kernel(height, got, index, done, out):
    scores, tails = unit_scores(height, got, index)
    tiles = index.shape[0] // LANES
    for i in range(out.shape[0]):
        for c in range(tiles):
            at = 2 * c * height
            out[i, at : at + height] = done[i, c * height : (c + 1) * height]
            rows = scores[i * height : (i + 1) * height, c * LANES : (c + 1) * LANES]
            out[i, at + height : at + 2 * height] = rows
        out[i, 2 * tiles * height :] = done[i, tiles * height :] + pltpu.roll(tails[i], height, 1)


def combine(tiles, height, factor, got):
    tails = [[down(block[tiles * height + t : tiles * height + t + 1], height) for t in range(4)] for block in got]
    top = tails[0][0]
    for tail in tails[1:]:
        top = jnp.maximum(top, tail[0])
    total, squares = [0.0] * tiles, 0.0
    for block, (g, *parts) in zip(got, tails):
        scale = jnp.exp2(g - top)
        squares += sum(parts) * (scale * scale)
        scale = scale * factor
        total = [total[c] + block[c * height : (c + 1) * height] * scale for c in range(tiles)]
    return total, squares, top


def last_kernel(me, got, out):
    height, tiles = out.shape[1], out.shape[2] // LANES
    total, squares, top = combine(tiles, 2 * height, 0.125, [got.at[i] for i in range(got.shape[0])])
    norm = jnp.sqrt(squares + 1e-06 * jnp.exp2(-2.0 * jnp.maximum(top, -60.0)))
    for c in range(tiles):
        block = total[c] / norm
        out[me[0], :, c * LANES : (c + 1) * LANES] = block[:height]
        out[1 - me[0], :, c * LANES : (c + 1) * LANES] = block[height:]


def call(kernel, spaces, shape, dtype, *args, **kwargs):
    return pl.pallas_call(
        kernel,
        out_shape=jax.ShapeDtypeStruct(shape, dtype),
        in_specs=[pl.BlockSpec(memory_space=space) for space in spaces],
        out_specs=pl.BlockSpec(memory_space=VMEM),
        compiler_params=pltpu.CompilerParams(vmem_limit_bytes=16 << 20),
        **kwargs,
    )(*args)


def swap(array):
    return lax.ppermute(array, "k", [(0, 1), (1, 0)])


def local(sizes, query, fisher, index):
    zh, x, zl, y, k = (sizes[a] for a in AXES)
    rows, pairs = zh * x, zl * y
    me = lax.axis_index("k").astype(jnp.int32).reshape(1)
    fisher_other = swap(fisher)
    height, width = query.shape[0] // k, query.shape[1]
    features, count = fisher.shape[0], index.shape[0]
    deep = features // LANES * height + TAIL
    short = count // LANES * height + TAIL
    wide = short * 2 - TAIL

    def exchange(sent, axes, shape):
        return lax.all_to_all(sent.reshape(-1, LANES), axes, 0, 0, tiled=True).reshape(shape)

    copies = call(copy_kernel, (VMEM,), (rows,) + query.shape, BF16, query).reshape(-1, width)
    held = lax.all_to_all(copies, ("x", "zh", "k"), 0, 0, tiled=True)
    held = held.reshape(rows, k, height, width)

    sent = call(
        first_kernel, (SMEM, VMEM, VMEM, VMEM), (pairs, deep, LANES), F32,
        me, held, fisher, fisher_other,
    )
    got = exchange(sent.astype(F16), PAIR, (pairs, deep, LANES)).astype(F32)

    sent = call(functools.partial(unit_kernel, height), (VMEM,), got.shape, BF16, got)
    got = exchange(sent, PAIR, got.shape)

    others = swap(got)
    cost = pl.CostEstimate(flops=2 * rows * height * count * features, bytes_accessed=8 << 20, transcendentals=0)
    kernel = functools.partial(score_kernel, height)
    done = call(kernel, (VMEM, VMEM), (rows, short, LANES), F32, got, index, cost_estimate=cost)
    kernel = functools.partial(rest_kernel, height)
    sent = call(kernel, (VMEM,) * 3, (rows, wide, LANES), F32, others, index, done, cost_estimate=cost)

    got = exchange(sent.astype(F16), ("x", "zh"), sent.shape).astype(F32)
    return call(last_kernel, (SMEM, VMEM), (k, height, count), F32, me, got).reshape(k * height, count)


def fine_mesh(mesh):
    rows, cols = mesh.devices.shape
    shape = (rows // 4, 4, 2, cols // 4, 2) if rows >= 16 else (2, rows // 2, 2, cols // 4, 2)
    return Mesh(mesh.devices.reshape(shape), AXES)


def solution(mesh):
    fine = fine_mesh(mesh)
    sizes = dict(fine.shape)
    row, col = ROW, (*PAIR, "k")
    placed = (P(row, col), P(row, col), P(col, row))
    return jax.shard_map(
        functools.partial(local, sizes), mesh=fine, in_specs=placed, out_specs=P(row, col), check_vma=False
    )
```

```python
import functools

import jax
import jax.numpy as jnp
from jax import lax
from jax.experimental import pallas as pl
from jax.experimental.pallas import tpu as pltpu
from jax.sharding import Mesh, PartitionSpec as P

F32, F16, BF16 = jnp.float32, jnp.float16, jnp.bfloat16
AXES = ("zh", "x", "zl", "y", "k")
ROW = ("zh", "x")
PAIR = ("zl", "y")
LANES = 128
TAIL = 8
MARKS = {"parts": 3, "over_x": 5, "over_zh": 7}
VMEM, SMEM = pltpu.VMEM, pltpu.SMEM


def exponent(rows):
    top = jnp.max(jnp.abs(rows), axis=-1, keepdims=True)
    return jnp.clip(jnp.ceil(jnp.log2(jnp.maximum(top, 1e-30))), -100.0, 100.0)


def diagonal(height):
    return lax.broadcasted_iota(jnp.int32, (height, LANES), 0) == lax.broadcasted_iota(jnp.int32, (height, LANES), 1)


def across(*columns):
    here = diagonal(columns[0].shape[0])
    row = lax.broadcasted_iota(jnp.int32, (TAIL, LANES), 0)
    out = jnp.zeros((TAIL, LANES), F32)
    for place, column in enumerate(columns):
        out = jnp.where(row == place, jnp.sum(jnp.where(here, column, 0.0), axis=0, keepdims=True), out)
    return out


def down(row, height):
    return jnp.sum(jnp.where(diagonal(height), row, 0.0), axis=1, keepdims=True)


def pieces(value):
    out = []
    for _ in range(3):
        out.append(value.astype(BF16).astype(F32))
        value = value - out[-1]
    return out


def dot_t(a, b):
    return lax.dot_general(a, b, (((1,), (1,)), ((), ())), preferred_element_type=F32)


def copy_kernel(query, out):
    for i in range(out.shape[0]):
        out[i] = query[...]


def first_kernel(order, me, held, fisher, other, out):
    core = me[0]
    groups, _, height, width = held.shape
    mine = held[:, core].reshape(groups * height, width)
    theirs = held[:, 1 - core].reshape(groups * height, width)
    part = dot_t(mine, fisher[...]) + dot_t(theirs, other[...])
    tiles = part.shape[1] // LANES
    e = exponent(part)
    part = part * jnp.exp2(12.0 - e)
    for to, source in enumerate(order):
        rows = slice(source * height, (source + 1) * height)
        for c in range(tiles):
            out[to, c * height : (c + 1) * height] = part[rows, c * LANES : (c + 1) * LANES]
        out[to, tiles * height :] = across(e[rows])


def unit_kernel(height, mark, got, out):
    tiles = (out.shape[1] - TAIL) // height
    full = [jnp.zeros((height, LANES), F32)] * tiles
    for i in range(got.shape[0]):
        scale = jnp.exp2(down(got[i, tiles * height : tiles * height + 1], height) - 12.0)
        full = [full[c] + got[i, c * height : (c + 1) * height] * scale for c in range(tiles)]
    full = jnp.concatenate(full, axis=1)
    g = exponent(full)
    unit = full * jnp.exp2(-g)
    squares = jnp.sum(unit * unit, axis=-1, keepdims=True)
    unit = unit.astype(BF16)
    tail = across(g, *pieces(squares)).astype(BF16)
    for copy in range(out.shape[0]):
        for c in range(tiles):
            out[copy, c * height : (c + 1) * height] = unit[:, c * LANES : (c + 1) * LANES]
        out[copy, tiles * height :] = tail


def score_kernel(height, got, index, other, out, held, sem):
    count, features = index.shape
    copy = pltpu.make_async_copy(other, held, sem)
    copy.start()
    sources, tiles = got.shape[0], features // LANES
    unit = jnp.concatenate(
        [got[:, c * height : (c + 1) * height].reshape(sources * height, LANES) for c in range(tiles)], axis=1
    )
    tails = got[:, tiles * height :].astype(F32)
    chunks = out.shape[0]
    per = sources // chunks
    rows = per * height
    tiles = count // LANES
    for i in range(chunks):
        tail = tails[i * per]
        for z in range(1, per):
            tail += pltpu.roll(tails[i * per + z], z * height, 1)
        out[i, 2 * tiles * rows :] = tail

    def put(block, scores):
        for i in range(chunks):
            for c in range(tiles):
                at = (block * tiles + c) * rows
                out[i, at : at + rows] = scores[i * rows : (i + 1) * rows, c * LANES : (c + 1) * LANES]

    put(0, dot_t(unit, index[...]) * 8.0)
    copy.wait()
    put(1, dot_t(unit, held[...]) * 8.0)


def combine(tiles, height, factor, got):
    tails = [[down(block[tiles * height + t : tiles * height + t + 1], height) for t in range(4)] for block in got]
    top = tails[0][0]
    for tail in tails[1:]:
        top = jnp.maximum(top, tail[0])
    total, squares = [0.0] * tiles, 0.0
    for block, (g, *parts) in zip(got, tails):
        scale = jnp.exp2(g - top)
        squares += sum(parts) * (scale * scale)
        scale = scale * factor
        total = [total[c] + block[c * height : (c + 1) * height] * scale for c in range(tiles)]
    return total, squares, top


def middle_kernel(height, mark, got, out):
    core = mark[0] - MARKS["over_x"]
    groups = out.shape[0]
    rows = groups * height
    tiles = (out.shape[2] - TAIL) // height
    total, squares, top = combine(2 * tiles, rows, 0.25, [got.at[i] for i in range(got.shape[0])])
    values = (top, *pieces(squares))
    for z in range(groups):
        here = slice(z * height, (z + 1) * height)
        tail = across(*(value[here] for value in values))
        for block, k in enumerate((core, 1 - core)):
            for c in range(tiles):
                out[z, k, c * height : (c + 1) * height] = total[block * tiles + c][here]
            out[z, k, tiles * height :] = tail


def last_kernel(height, mark, got, out):
    tiles = out.shape[1] // LANES
    for k in range(got.shape[1]):
        total, squares, top = combine(tiles, height, 0.5, [got.at[i, k] for i in range(got.shape[0])])
        norm = jnp.sqrt(squares + 1e-06 * jnp.exp2(-2.0 * jnp.maximum(top, -60.0)))
        for c in range(tiles):
            out[k * height : (k + 1) * height, c * LANES : (c + 1) * LANES] = total[c] / norm


def call(kernel, spaces, shape, dtype, *args, **kwargs):
    return pl.pallas_call(
        kernel,
        out_shape=jax.ShapeDtypeStruct(shape, dtype),
        in_specs=[pl.BlockSpec(memory_space=space) for space in spaces],
        out_specs=pl.BlockSpec(memory_space=VMEM),
        compiler_params=pltpu.CompilerParams(vmem_limit_bytes=16 << 20),
        **kwargs,
    )(*args)


def mark(name, me):
    def kernel(me, out):
        out[0] = me[0] + MARKS[name]

    return pl.pallas_call(
        kernel,
        out_shape=jax.ShapeDtypeStruct((1,), jnp.int32),
        in_specs=[pl.BlockSpec(memory_space=SMEM)],
        out_specs=pl.BlockSpec(memory_space=SMEM),
        cost_estimate=pl.CostEstimate(flops=1, bytes_accessed=8, transcendentals=0),
    )(me)


def swap(array):
    return lax.ppermute(array, "k", [(0, 1), (1, 0)])


def local(sizes, query, fisher, index):
    zh, x, zl, y, k = (sizes[a] for a in AXES)
    rows, pairs = zh * x, zl * y
    me = lax.axis_index("k").astype(jnp.int32).reshape(1)
    fisher_other = swap(fisher)
    index_other = swap(index)
    height, width = query.shape[0] // k, query.shape[1]
    features, count = fisher.shape[0], index.shape[0]
    deep = features // LANES * height + TAIL
    wide = 2 * (count // LANES) * zh * height + TAIL
    short = count // LANES * height + TAIL

    def exchange(sent, axes, shape):
        return lax.all_to_all(sent.reshape(-1, LANES), axes, 0, 0, tiled=True).reshape(shape)

    copies = call(copy_kernel, (VMEM,), (rows,) + query.shape, BF16, query).reshape(-1, width)
    held = lax.all_to_all(copies, (*ROW, "k"), 0, 0, tiled=True)
    held = held.reshape(rows, k, height, width)

    order = tuple(z * x + i for i in range(x) for z in range(zh))
    sent = call(
        functools.partial(first_kernel, order), (SMEM, VMEM, VMEM, VMEM), (pairs, deep, LANES), F32,
        me, held, fisher, fisher_other,
    )
    sent = sent.astype(F16)
    got = exchange(sent, PAIR, (pairs, deep, LANES))
    got = got.astype(F32)

    kernel = functools.partial(unit_kernel, height)
    sent = call(kernel, (SMEM, VMEM), got.shape, BF16, mark("parts", me), got)
    got = exchange(sent, PAIR, got.shape)

    sent = call(
        functools.partial(score_kernel, height), (VMEM, VMEM, pl.ANY), (x, wide, LANES), F32, got, index, index_other,
        scratch_shapes=[VMEM((count, features), BF16), pltpu.SemaphoreType.DMA],
    )
    sent = sent.astype(F16)
    got = exchange(sent, "x", sent.shape)
    got = got.astype(F32)

    kernel = functools.partial(middle_kernel, height)
    sent = call(kernel, (SMEM, VMEM), (zh, k, short, LANES), F32, mark("over_x", me), got)
    sent = sent.astype(F16)
    got = exchange(sent, ("zh", "k"), sent.shape)
    got = got.astype(F32)
    kernel = functools.partial(last_kernel, height)
    return call(kernel, (SMEM, VMEM), (k * height, count), F32, mark("over_zh", me), got)


def fine_mesh(mesh):
    rows, cols = mesh.devices.shape
    shape = (rows // 4, 4, 2, cols // 4, 2) if rows >= 16 else (2, rows // 2, 2, cols // 4, 2)
    return Mesh(mesh.devices.reshape(shape), AXES)


def solution(mesh):
    fine = fine_mesh(mesh)
    sizes = dict(fine.shape)
    row, col = ROW, (*PAIR, "k")
    placed = (P(row, col), P(row, col), P(col, row))
    return jax.shard_map(
        functools.partial(local, sizes), mesh=fine, in_specs=placed, out_specs=P(row, col), check_vma=False
    )
```

```python
import functools

import jax
import jax.numpy as jnp
from jax import lax
from jax.experimental import pallas as pl
from jax.experimental.pallas import tpu as pltpu
from jax.sharding import Mesh, PartitionSpec as P

F32, F16, BF16 = jnp.float32, jnp.float16, jnp.bfloat16
AXES = ("zh", "x", "zl", "y", "k")
ROW = ("zh", "x")
PAIR = ("zl", "y")
LANES = 128
TAIL = 8
VMEM, SMEM = pltpu.VMEM, pltpu.SMEM


def exponent(rows):
    top = jnp.max(jnp.abs(rows), axis=-1, keepdims=True)
    return jnp.clip(jnp.ceil(jnp.log2(jnp.maximum(top, 1e-30))), -100.0, 100.0)


def diagonal(height):
    return lax.broadcasted_iota(jnp.int32, (height, LANES), 0) == lax.broadcasted_iota(jnp.int32, (height, LANES), 1)


def across(*columns):
    here = diagonal(columns[0].shape[0])
    row = lax.broadcasted_iota(jnp.int32, (TAIL, LANES), 0)
    out = jnp.zeros((TAIL, LANES), F32)
    for place, column in enumerate(columns):
        out = jnp.where(row == place, jnp.sum(jnp.where(here, column, 0.0), axis=0, keepdims=True), out)
    return out


def down(row, height):
    return jnp.sum(jnp.where(diagonal(height), row, 0.0), axis=1, keepdims=True)


def pieces(value):
    out = []
    for _ in range(3):
        out.append(value.astype(BF16).astype(F32))
        value = value - out[-1]
    return out


def dot_t(a, b):
    return lax.dot_general(a, b, (((1,), (1,)), ((), ())), preferred_element_type=F32)


def copy_kernel(query, out):
    for i in range(out.shape[0]):
        out[i] = query[...]


def first_kernel(order, me, held, fisher, other, out):
    core = me[0]
    groups, _, height, width = held.shape
    mine = held[:, core].reshape(groups * height, width)
    theirs = held[:, 1 - core].reshape(groups * height, width)
    part = dot_t(mine, fisher[...]) + dot_t(theirs, other[...])
    tiles = part.shape[1] // LANES
    e = exponent(part)
    part = part * jnp.exp2(12.0 - e)
    for to, source in enumerate(order):
        rows = slice(source * height, (source + 1) * height)
        for c in range(tiles):
            out[to, c * height : (c + 1) * height] = part[rows, c * LANES : (c + 1) * LANES]
        out[to, tiles * height :] = across(e[rows])


def unit_kernel(height, got, out):
    tiles = (out.shape[1] - TAIL) // height
    full = [jnp.zeros((height, LANES), F32)] * tiles
    for i in range(got.shape[0]):
        scale = jnp.exp2(down(got[i, tiles * height : tiles * height + 1], height) - 12.0)
        full = [full[c] + got[i, c * height : (c + 1) * height] * scale for c in range(tiles)]
    full = jnp.concatenate(full, axis=1)
    g = exponent(full)
    unit = full * jnp.exp2(-g)
    squares = jnp.sum(unit * unit, axis=-1, keepdims=True)
    unit = unit.astype(BF16)
    tail = across(g, *pieces(squares)).astype(BF16)
    for copy in range(out.shape[0]):
        for c in range(tiles):
            out[copy, c * height : (c + 1) * height] = unit[:, c * LANES : (c + 1) * LANES]
        out[copy, tiles * height :] = tail


def score_kernel(height, got, index, other, out, held, sem):
    count, features = index.shape
    copy = pltpu.make_async_copy(other, held, sem)
    copy.start()
    sources, tiles = got.shape[0], features // LANES
    unit = jnp.concatenate(
        [got[:, c * height : (c + 1) * height].reshape(sources * height, LANES) for c in range(tiles)], axis=1
    )
    tails = got[:, tiles * height :].astype(F32)
    chunks = out.shape[0]
    per = sources // chunks
    rows = per * height
    tiles = count // LANES
    for i in range(chunks):
        tail = tails[i * per]
        for z in range(1, per):
            tail += pltpu.roll(tails[i * per + z], z * height, 1)
        out[i, 2 * tiles * rows :] = tail

    def put(block, scores):
        for i in range(chunks):
            for c in range(tiles):
                at = (block * tiles + c) * rows
                out[i, at : at + rows] = scores[i * rows : (i + 1) * rows, c * LANES : (c + 1) * LANES]

    put(0, dot_t(unit, index[...]) * 8.0)
    copy.wait()
    put(1, dot_t(unit, held[...]) * 8.0)


def combine(tiles, height, factor, got):
    tails = [[down(block[tiles * height + t : tiles * height + t + 1], height) for t in range(4)] for block in got]
    top = tails[0][0]
    for tail in tails[1:]:
        top = jnp.maximum(top, tail[0])
    total, squares = [0.0] * tiles, 0.0
    for block, (g, *parts) in zip(got, tails):
        scale = jnp.exp2(g - top)
        squares += sum(parts) * (scale * scale)
        scale = scale * factor
        total = [total[c] + block[c * height : (c + 1) * height] * scale for c in range(tiles)]
    return total, squares, top


def middle_kernel(height, me, got, out):
    groups = out.shape[0]
    rows = groups * height
    tiles = (out.shape[2] - TAIL) // height
    total, squares, top = combine(2 * tiles, rows, 0.25, [got.at[i] for i in range(got.shape[0])])
    values = (top, *pieces(squares))
    for z in range(groups):
        here = slice(z * height, (z + 1) * height)
        tail = across(*(value[here] for value in values))
        for block, k in enumerate((me[0], 1 - me[0])):
            for c in range(tiles):
                out[z, k, c * height : (c + 1) * height] = total[block * tiles + c][here]
            out[z, k, tiles * height :] = tail


def last_kernel(height, got, out):
    tiles = out.shape[1] // LANES
    for k in range(got.shape[1]):
        total, squares, top = combine(tiles, height, 0.5, [got.at[i, k] for i in range(got.shape[0])])
        norm = jnp.sqrt(squares + 1e-06 * jnp.exp2(-2.0 * jnp.maximum(top, -60.0)))
        for c in range(tiles):
            out[k * height : (k + 1) * height, c * LANES : (c + 1) * LANES] = total[c] / norm


def call(kernel, spaces, shape, dtype, *args, **kwargs):
    return pl.pallas_call(
        kernel,
        out_shape=jax.ShapeDtypeStruct(shape, dtype),
        in_specs=[pl.BlockSpec(memory_space=space) for space in spaces],
        out_specs=pl.BlockSpec(memory_space=VMEM),
        compiler_params=pltpu.CompilerParams(vmem_limit_bytes=16 << 20),
        **kwargs,
    )(*args)


def beside(me):
    def kernel(me, out):
        out[0] = me[0] + 1

    pl.pallas_call(
        kernel,
        out_shape=jax.ShapeDtypeStruct((1,), jnp.int32),
        in_specs=[pl.BlockSpec(memory_space=SMEM)],
        out_specs=pl.BlockSpec(memory_space=SMEM),
        compiler_params=pltpu.CompilerParams(has_side_effects=True),
    )(me)


def swap(array):
    return lax.ppermute(array, "k", [(0, 1), (1, 0)])


def local(sizes, query, fisher, index):
    zh, x, zl, y, k = (sizes[a] for a in AXES)
    rows, pairs = zh * x, zl * y
    me = lax.axis_index("k").astype(jnp.int32).reshape(1)
    fisher_other = swap(fisher)
    index_other = swap(index)
    height, width = query.shape[0] // k, query.shape[1]
    features, count = fisher.shape[0], index.shape[0]
    deep = features // LANES * height + TAIL
    wide = 2 * (count // LANES) * zh * height + TAIL
    short = count // LANES * height + TAIL

    def exchange(sent, axes, shape):
        return lax.all_to_all(sent.reshape(-1, LANES), axes, 0, 0, tiled=True).reshape(shape)

    copies = call(copy_kernel, (VMEM,), (rows,) + query.shape, BF16, query).reshape(-1, width)
    held = lax.all_to_all(copies, (*ROW, "k"), 0, 0, tiled=True)
    held = held.reshape(rows, k, height, width)

    order = tuple(z * x + i for i in range(x) for z in range(zh))
    sent = call(
        functools.partial(first_kernel, order), (SMEM, VMEM, VMEM, VMEM), (pairs, deep, LANES), F32,
        me, held, fisher, fisher_other,
    )
    got = exchange(sent.astype(F16), PAIR, (pairs, deep, LANES)).astype(F32)

    sent = call(functools.partial(unit_kernel, height), (VMEM,), got.shape, BF16, got)
    got = exchange(sent, PAIR, got.shape)

    sent = call(
        functools.partial(score_kernel, height), (VMEM, VMEM, pl.ANY), (x, wide, LANES), F32, got, index, index_other,
        scratch_shapes=[VMEM((count, features), BF16), pltpu.SemaphoreType.DMA],
    )
    got = exchange(sent.astype(F16), "x", sent.shape).astype(F32)

    sent = call(functools.partial(middle_kernel, height), (SMEM, VMEM), (zh, k, short, LANES), F32, me, got)
    sent = sent.astype(F16)
    got = exchange(sent, ("zh", "k"), sent.shape)
    beside(me)
    got = got.astype(F32)
    return call(functools.partial(last_kernel, height), (VMEM,), (k * height, count), F32, got)


def fine_mesh(mesh):
    rows, cols = mesh.devices.shape
    shape = (rows // 4, 4, 2, cols // 4, 2) if rows >= 16 else (2, rows // 2, 2, cols // 4, 2)
    return Mesh(mesh.devices.reshape(shape), AXES)


def solution(mesh):
    fine = fine_mesh(mesh)
    sizes = dict(fine.shape)
    row, col = ROW, (*PAIR, "k")
    placed = (P(row, col), P(row, col), P(col, row))
    return jax.shard_map(
        functools.partial(local, sizes), mesh=fine, in_specs=placed, out_specs=P(row, col), check_vma=False
    )
```

```python
import functools

import jax
import jax.numpy as jnp
from jax import lax
from jax.experimental import pallas as pl
from jax.experimental.pallas import tpu as pltpu
from jax.sharding import Mesh, PartitionSpec as P

F32, F16, BF16 = jnp.float32, jnp.float16, jnp.bfloat16
AXES = ("zh", "x", "zl", "y", "k")
ROW = ("zh", "x")
PAIR = ("zl", "y")
LANES = 128
TAIL = 8
VMEM, SMEM = pltpu.VMEM, pltpu.SMEM


def exponent(rows):
    top = jnp.max(jnp.abs(rows), axis=-1, keepdims=True)
    return jnp.clip(jnp.ceil(jnp.log2(jnp.maximum(top, 1e-30))), -100.0, 100.0)


def diagonal(height):
    return lax.broadcasted_iota(jnp.int32, (height, LANES), 0) == lax.broadcasted_iota(jnp.int32, (height, LANES), 1)


def across(*columns):
    here = diagonal(columns[0].shape[0])
    row = lax.broadcasted_iota(jnp.int32, (TAIL, LANES), 0)
    out = jnp.zeros((TAIL, LANES), F32)
    for place, column in enumerate(columns):
        out = jnp.where(row == place, jnp.sum(jnp.where(here, column, 0.0), axis=0, keepdims=True), out)
    return out


def down(row, height):
    return jnp.sum(jnp.where(diagonal(height), row, 0.0), axis=1, keepdims=True)


def pieces(value):
    out = []
    for _ in range(3):
        out.append(value.astype(BF16).astype(F32))
        value = value - out[-1]
    return out


def dot_t(a, b):
    return lax.dot_general(a, b, (((1,), (1,)), ((), ())), preferred_element_type=F32)


def copy_kernel(query, out):
    for i in range(out.shape[0]):
        out[i] = query[...]


def first_kernel(order, me, held, fisher, other, out):
    core = me[0]
    groups, _, height, width = held.shape
    mine = held[:, core].reshape(groups * height, width)
    theirs = held[:, 1 - core].reshape(groups * height, width)
    part = dot_t(mine, fisher[...]) + dot_t(theirs, other[...])
    tiles = part.shape[1] // LANES
    e = exponent(part)
    part = part * jnp.exp2(12.0 - e)
    for to, source in enumerate(order):
        rows = slice(source * height, (source + 1) * height)
        for c in range(tiles):
            out[to, c * height : (c + 1) * height] = part[rows, c * LANES : (c + 1) * LANES]
        out[to, tiles * height :] = across(e[rows])


def unit_kernel(height, got, out):
    tiles = (out.shape[1] - TAIL) // height
    full = [jnp.zeros((height, LANES), F32)] * tiles
    for i in range(got.shape[0]):
        scale = jnp.exp2(down(got[i, tiles * height : tiles * height + 1], height) - 12.0)
        full = [full[c] + got[i, c * height : (c + 1) * height] * scale for c in range(tiles)]
    full = jnp.concatenate(full, axis=1)
    g = exponent(full)
    unit = full * jnp.exp2(-g)
    squares = jnp.sum(unit * unit, axis=-1, keepdims=True)
    unit = unit.astype(BF16)
    tail = across(g, *pieces(squares)).astype(BF16)
    for copy in range(out.shape[0]):
        for c in range(tiles):
            out[copy, c * height : (c + 1) * height] = unit[:, c * LANES : (c + 1) * LANES]
        out[copy, tiles * height :] = tail


def score_kernel(height, got, index, other, out, held, sems):
    count, features = index.shape
    depth = count // sems.shape[0]
    copies = [
        pltpu.make_async_copy(other.at[pl.ds(i * depth, depth)], held.at[pl.ds(i * depth, depth)], sems.at[i])
        for i in range(sems.shape[0])
    ]
    for copy in copies:
        copy.start()
    sources, tiles = got.shape[0], features // LANES
    unit = jnp.concatenate(
        [got[:, c * height : (c + 1) * height].reshape(sources * height, LANES) for c in range(tiles)], axis=1
    )
    tails = got[:, tiles * height :].astype(F32)
    chunks = out.shape[0]
    per = sources // chunks
    rows = per * height
    tiles = count // LANES
    for i in range(chunks):
        tail = tails[i * per]
        for z in range(1, per):
            tail += pltpu.roll(tails[i * per + z], z * height, 1)
        out[i, 2 * tiles * rows :] = tail

    def put(first, scores):
        for i in range(chunks):
            for c in range(scores.shape[1] // LANES):
                at = (first + c) * rows
                out[i, at : at + rows] = scores[i * rows : (i + 1) * rows, c * LANES : (c + 1) * LANES]

    put(0, dot_t(unit, index[...]) * 8.0)
    for i, copy in enumerate(copies):
        copy.wait()
        put(tiles + i * depth // LANES, dot_t(unit, held[i * depth : (i + 1) * depth]) * 8.0)


def combine(tiles, height, factor, got):
    tails = [[down(block[tiles * height + t : tiles * height + t + 1], height) for t in range(4)] for block in got]
    top = tails[0][0]
    for tail in tails[1:]:
        top = jnp.maximum(top, tail[0])
    total, squares = [0.0] * tiles, 0.0
    for block, (g, *parts) in zip(got, tails):
        scale = jnp.exp2(g - top)
        squares += sum(parts) * (scale * scale)
        scale = scale * factor
        total = [total[c] + block[c * height : (c + 1) * height] * scale for c in range(tiles)]
    return total, squares, top


def middle_kernel(height, me, got, out):
    groups = out.shape[0]
    rows = groups * height
    tiles = (out.shape[2] - TAIL) // height
    total, squares, top = combine(2 * tiles, rows, 0.25, [got.at[i] for i in range(got.shape[0])])
    values = (top, *pieces(squares))
    for z in range(groups):
        here = slice(z * height, (z + 1) * height)
        tail = across(*(value[here] for value in values))
        for block, k in enumerate((me[0], 1 - me[0])):
            for c in range(tiles):
                out[z, k, c * height : (c + 1) * height] = total[block * tiles + c][here]
            out[z, k, tiles * height :] = tail


def last_kernel(height, got, out):
    tiles = out.shape[1] // LANES
    for k in range(got.shape[1]):
        total, squares, top = combine(tiles, height, 0.5, [got.at[i, k] for i in range(got.shape[0])])
        norm = jnp.sqrt(squares + 1e-06 * jnp.exp2(-2.0 * jnp.maximum(top, -60.0)))
        for c in range(tiles):
            out[k * height : (k + 1) * height, c * LANES : (c + 1) * LANES] = total[c] / norm


def call(kernel, spaces, shape, dtype, *args, **kwargs):
    return pl.pallas_call(
        kernel,
        out_shape=jax.ShapeDtypeStruct(shape, dtype),
        in_specs=[pl.BlockSpec(memory_space=space) for space in spaces],
        out_specs=pl.BlockSpec(memory_space=VMEM),
        compiler_params=pltpu.CompilerParams(vmem_limit_bytes=16 << 20),
        **kwargs,
    )(*args)


def swap(array):
    return lax.ppermute(array, "k", [(0, 1), (1, 0)])


def local(sizes, query, fisher, index):
    zh, x, zl, y, k = (sizes[a] for a in AXES)
    rows, pairs = zh * x, zl * y
    me = lax.axis_index("k").astype(jnp.int32).reshape(1)
    fisher_other = swap(fisher)
    index_other = swap(index)
    height, width = query.shape[0] // k, query.shape[1]
    features, count = fisher.shape[0], index.shape[0]
    deep = features // LANES * height + TAIL
    wide = 2 * (count // LANES) * zh * height + TAIL
    short = count // LANES * height + TAIL

    def exchange(sent, axes, shape):
        return lax.all_to_all(sent.reshape(-1, LANES), axes, 0, 0, tiled=True).reshape(shape)

    copies = call(copy_kernel, (VMEM,), (rows,) + query.shape, BF16, query).reshape(-1, width)
    held = lax.all_to_all(copies, (*ROW, "k"), 0, 0, tiled=True)
    held = held.reshape(rows, k, height, width)

    order = tuple(z * x + i for i in range(x) for z in range(zh))
    sent = call(
        functools.partial(first_kernel, order), (SMEM, VMEM, VMEM, VMEM), (pairs, deep, LANES), F32,
        me, held, fisher, fisher_other,
    )
    got = exchange(sent.astype(F16), PAIR, (pairs, deep, LANES)).astype(F32)

    sent = call(functools.partial(unit_kernel, height), (VMEM,), got.shape, BF16, got)
    got = exchange(sent, PAIR, got.shape)

    sent = call(
        functools.partial(score_kernel, height), (VMEM, VMEM, pl.ANY), (x, wide, LANES), F32, got, index, index_other,
        scratch_shapes=[VMEM((count, features), BF16), pltpu.SemaphoreType.DMA((4,))],
    )
    got = exchange(sent.astype(F16), "x", sent.shape).astype(F32)

    sent = call(functools.partial(middle_kernel, height), (SMEM, VMEM), (zh, k, short, LANES), F32, me, got)
    got = exchange(sent.astype(F16), ("zh", "k"), sent.shape).astype(F32)
    return call(functools.partial(last_kernel, height), (VMEM,), (k * height, count), F32, got)


def fine_mesh(mesh):
    rows, cols = mesh.devices.shape
    shape = (rows // 4, 4, 2, cols // 4, 2) if rows >= 16 else (2, rows // 2, 2, cols // 4, 2)
    return Mesh(mesh.devices.reshape(shape), AXES)


def solution(mesh):
    fine = fine_mesh(mesh)
    sizes = dict(fine.shape)
    row, col = ROW, (*PAIR, "k")
    placed = (P(row, col), P(row, col), P(col, row))
    return jax.shard_map(
        functools.partial(local, sizes), mesh=fine, in_specs=placed, out_specs=P(row, col), check_vma=False
    )
```

```python
import functools

import jax
import jax.numpy as jnp
from jax import lax
from jax.experimental import pallas as pl
from jax.experimental.pallas import tpu as pltpu
from jax.sharding import Mesh, PartitionSpec as P

F32, F16, BF16 = jnp.float32, jnp.float16, jnp.bfloat16
AXES = ("zh", "x", "zl", "y", "k")
ROW = ("zh", "x")
PAIR = ("zl", "y")
LANES = 128
TAIL = 8
VMEM, SMEM = pltpu.VMEM, pltpu.SMEM


def exponent(rows):
    top = jnp.max(jnp.abs(rows), axis=-1, keepdims=True)
    return jnp.clip(jnp.ceil(jnp.log2(jnp.maximum(top, 1e-30))), -100.0, 100.0)


def diagonal(height):
    return lax.broadcasted_iota(jnp.int32, (height, LANES), 0) == lax.broadcasted_iota(jnp.int32, (height, LANES), 1)


def across(*columns):
    here = diagonal(columns[0].shape[0])
    row = lax.broadcasted_iota(jnp.int32, (TAIL, LANES), 0)
    out = jnp.zeros((TAIL, LANES), F32)
    for place, column in enumerate(columns):
        out = jnp.where(row == place, jnp.sum(jnp.where(here, column, 0.0), axis=0, keepdims=True), out)
    return out


def down(row, height):
    return jnp.sum(jnp.where(diagonal(height), row, 0.0), axis=1, keepdims=True)


def pieces(value):
    out = []
    for _ in range(3):
        out.append(value.astype(BF16).astype(F32))
        value = value - out[-1]
    return out


def dot_t(a, b):
    return lax.dot_general(a, b, (((1,), (1,)), ((), ())), preferred_element_type=F32)


def copy_kernel(query, out):
    for i in range(out.shape[0]):
        out[i] = query[...]


def first_kernel(order, me, held, fisher, other, out):
    core = me[0]
    groups, _, height, width = held.shape
    mine = held[:, core].reshape(groups * height, width)
    theirs = held[:, 1 - core].reshape(groups * height, width)
    part = dot_t(mine, fisher[...]) + dot_t(theirs, other[...])
    tiles = part.shape[1] // LANES
    e = exponent(part)
    part = part * jnp.exp2(12.0 - e)
    for to, source in enumerate(order):
        rows = slice(source * height, (source + 1) * height)
        for c in range(tiles):
            out[to, c * height : (c + 1) * height] = part[rows, c * LANES : (c + 1) * LANES]
        out[to, tiles * height :] = across(e[rows])


def unit_kernel(height, got, out, block, sems):
    tiles = (out.shape[1] - TAIL) // height
    full = [jnp.zeros((height, LANES), F32)] * tiles
    for i in range(got.shape[0]):
        scale = jnp.exp2(down(got[i, tiles * height : tiles * height + 1], height) - 12.0)
        full = [full[c] + got[i, c * height : (c + 1) * height] * scale for c in range(tiles)]
    full = jnp.concatenate(full, axis=1)
    g = exponent(full)
    unit = full * jnp.exp2(-g)
    squares = jnp.sum(unit * unit, axis=-1, keepdims=True)
    unit = unit.astype(BF16)
    tail = across(g, *pieces(squares)).astype(BF16)
    for c in range(tiles):
        block[c * height : (c + 1) * height] = unit[:, c * LANES : (c + 1) * LANES]
    block[tiles * height :] = tail
    copies = [pltpu.make_async_copy(block, out.at[i], sems.at[i]) for i in range(out.shape[0])]
    for copy in copies:
        copy.start()
    for copy in copies:
        copy.wait()


def score_kernel(height, got, index, other, out, held, sem):
    count, features = index.shape
    copy = pltpu.make_async_copy(other, held, sem)
    copy.start()
    sources, tiles = got.shape[0], features // LANES
    unit = jnp.concatenate(
        [got[:, c * height : (c + 1) * height].reshape(sources * height, LANES) for c in range(tiles)], axis=1
    )
    tails = got[:, tiles * height :].astype(F32)
    chunks = out.shape[0]
    per = sources // chunks
    rows = per * height
    tiles = count // LANES
    for i in range(chunks):
        tail = tails[i * per]
        for z in range(1, per):
            tail += pltpu.roll(tails[i * per + z], z * height, 1)
        out[i, 2 * tiles * rows :] = tail

    def put(block, scores):
        for i in range(chunks):
            for c in range(tiles):
                at = (block * tiles + c) * rows
                out[i, at : at + rows] = scores[i * rows : (i + 1) * rows, c * LANES : (c + 1) * LANES]

    put(0, dot_t(unit, index[...]) * 8.0)
    copy.wait()
    put(1, dot_t(unit, held[...]) * 8.0)


def combine(tiles, height, factor, got):
    tails = [[down(block[tiles * height + t : tiles * height + t + 1], height) for t in range(4)] for block in got]
    top = tails[0][0]
    for tail in tails[1:]:
        top = jnp.maximum(top, tail[0])
    total, squares = [0.0] * tiles, 0.0
    for block, (g, *parts) in zip(got, tails):
        scale = jnp.exp2(g - top)
        squares += sum(parts) * (scale * scale)
        scale = scale * factor
        total = [total[c] + block[c * height : (c + 1) * height] * scale for c in range(tiles)]
    return total, squares, top


def middle_kernel(height, me, got, out):
    groups = out.shape[0]
    rows = groups * height
    tiles = (out.shape[2] - TAIL) // height
    total, squares, top = combine(2 * tiles, rows, 0.25, [got.at[i] for i in range(got.shape[0])])
    values = (top, *pieces(squares))
    for z in range(groups):
        here = slice(z * height, (z + 1) * height)
        tail = across(*(value[here] for value in values))
        for block, k in enumerate((me[0], 1 - me[0])):
            for c in range(tiles):
                out[z, k, c * height : (c + 1) * height] = total[block * tiles + c][here]
            out[z, k, tiles * height :] = tail


def last_kernel(height, got, out):
    tiles = out.shape[1] // LANES
    for k in range(got.shape[1]):
        total, squares, top = combine(tiles, height, 0.5, [got.at[i, k] for i in range(got.shape[0])])
        norm = jnp.sqrt(squares + 1e-06 * jnp.exp2(-2.0 * jnp.maximum(top, -60.0)))
        for c in range(tiles):
            out[k * height : (k + 1) * height, c * LANES : (c + 1) * LANES] = total[c] / norm


def call(kernel, spaces, shape, dtype, *args, out_space=VMEM, **kwargs):
    return pl.pallas_call(
        kernel,
        out_shape=jax.ShapeDtypeStruct(shape, dtype),
        in_specs=[pl.BlockSpec(memory_space=space) for space in spaces],
        out_specs=pl.BlockSpec(memory_space=out_space),
        compiler_params=pltpu.CompilerParams(vmem_limit_bytes=16 << 20),
        **kwargs,
    )(*args)


def swap(array):
    return lax.ppermute(array, "k", [(0, 1), (1, 0)])


def local(sizes, query, fisher, index):
    zh, x, zl, y, k = (sizes[a] for a in AXES)
    rows, pairs = zh * x, zl * y
    me = lax.axis_index("k").astype(jnp.int32).reshape(1)
    fisher_other = swap(fisher)
    index_other = swap(index)
    height, width = query.shape[0] // k, query.shape[1]
    features, count = fisher.shape[0], index.shape[0]
    deep = features // LANES * height + TAIL
    wide = 2 * (count // LANES) * zh * height + TAIL
    short = count // LANES * height + TAIL

    def exchange(sent, axes, shape):
        return lax.all_to_all(sent.reshape(-1, LANES), axes, 0, 0, tiled=True).reshape(shape)

    copies = call(copy_kernel, (VMEM,), (rows,) + query.shape, BF16, query).reshape(-1, width)
    held = lax.all_to_all(copies, (*ROW, "k"), 0, 0, tiled=True)
    held = held.reshape(rows, k, height, width)

    order = tuple(z * x + i for i in range(x) for z in range(zh))
    sent = call(
        functools.partial(first_kernel, order), (SMEM, VMEM, VMEM, VMEM), (pairs, deep, LANES), F32,
        me, held, fisher, fisher_other,
    )
    got = exchange(sent.astype(F16), PAIR, (pairs, deep, LANES)).astype(F32)

    sent = call(
        functools.partial(unit_kernel, height), (VMEM,), got.shape, BF16, got, out_space=pl.ANY,
        scratch_shapes=[VMEM((deep, LANES), BF16), pltpu.SemaphoreType.DMA((pairs,))],
    )
    got = exchange(sent, PAIR, got.shape)

    sent = call(
        functools.partial(score_kernel, height), (VMEM, VMEM, pl.ANY), (x, wide, LANES), F32, got, index, index_other,
        scratch_shapes=[VMEM((count, features), BF16), pltpu.SemaphoreType.DMA],
    )
    got = exchange(sent.astype(F16), "x", sent.shape).astype(F32)

    sent = call(functools.partial(middle_kernel, height), (SMEM, VMEM), (zh, k, short, LANES), F32, me, got)
    got = exchange(sent.astype(F16), ("zh", "k"), sent.shape).astype(F32)
    return call(functools.partial(last_kernel, height), (VMEM,), (k * height, count), F32, got)


def fine_mesh(mesh):
    rows, cols = mesh.devices.shape
    shape = (rows // 4, 4, 2, cols // 4, 2) if rows >= 16 else (2, rows // 2, 2, cols // 4, 2)
    return Mesh(mesh.devices.reshape(shape), AXES)


def solution(mesh):
    fine = fine_mesh(mesh)
    sizes = dict(fine.shape)
    row, col = ROW, (*PAIR, "k")
    placed = (P(row, col), P(row, col), P(col, row))
    return jax.shard_map(
        functools.partial(local, sizes), mesh=fine, in_specs=placed, out_specs=P(row, col), check_vma=False
    )
```
